32 devices in a mesh: member: 4 (over y, x), space: 8 (over z, core).
Axes of the slice: x: 2, y: 2, z: 4, core: 2. Of those that a mesh axis runs over, the one named last changes fastest.
Arguments:
- features: bfloat16 [8, 32, 64, 1024], P('member', None, 'space'), may hold values from -6 to 6
- skip: bfloat16 [8, 32, 64, 1024], P('member', None, 'space'), may hold values from -6 to 6
- conv_weight: bfloat16 [3, 3, 32, 32], replicated, may hold values from -0.625 to 0.625
- out_weight: bfloat16 [2, 32], replicated, may hold values from -2 to 2
- target: float32 [2, 64, 1024], P(None, 'space'), may hold values from -12 to 12
Outputs:
- grad_input: bfloat16 [8, 32, 64, 1024], P('member', None, 'space')
The draws below stay inside these ranges and needn't reach their ends.
All inputs are finite; a program needn't handle non-finite values.
Results may differ from the reference program's by a relative error of at most 0.012.
Values may be sent and summed in bfloat16 or wider, within the bound.
A program may use at most 64 MiB of HBM per device.

```python
import math
import jax
import jax.numpy as jnp
from jax import lax

C = 32
OUT = 2
COLS = 1024
MEMBERS = 8
ROWS = 64


def levels(stream_key, dims, cuts, smallest, top_value):
    def one(position, shards_of):
        steps = jax.random.uniform(jax.random.fold_in(jax.random.fold_in(stream_key, 6), position), (shards_of,), jnp.float32, smallest / len(cuts), top_value / len(cuts))
        return jnp.repeat(jnp.exp(steps), dims[position] // shards_of).reshape((-1,) + (1,) * (len(dims) - position - 1))

    gain = one(*cuts[0])
    for cut in cuts[1:]:
        gain = gain * one(*cut)
    return gain


def bell_draw(rng, dims, width, limit, split=(), dtype=jnp.bfloat16):
    values = width * jax.random.normal(rng, dims, jnp.float32)
    if split:
        values = values * levels(rng, dims, split, -0.22, 0.18)
    return jnp.clip(values, -limit, limit).astype(dtype)


def setup_inputs(seed: int = 0) -> dict:
    streams_of = jax.random.split(jax.random.key(seed), 6)
    features = bell_draw(streams_of[0], (MEMBERS, C, ROWS, COLS), 1.0, 6.0, ((0, 4), (2, 8)))
    skip = bell_draw(streams_of[1], (MEMBERS, C, ROWS, COLS), 1.0, 6.0, ((0, 4), (2, 8)))
    conv_weight = bell_draw(streams_of[2], (3, 3, C, C), (3 * C) ** -0.5, 0.625)
    out_weight = bell_draw(streams_of[3], (OUT, C), (C // 4) ** -0.5, 2.0)
    target = bell_draw(streams_of[4], (OUT, ROWS, COLS), 2.0, 12.0, ((1, 8),), jnp.float32)
    return dict(features=features, skip=skip, conv_weight=conv_weight, out_weight=out_weight, target=target)


root_coef = math.sqrt(2.0 / math.pi)
cubic_coef = 0.044715
smooth = 0.25

def gelu_value(source):
    inside = root_coef * (source + cubic_coef * source * source * source)
    return 0.5 * source * (1.0 + jnp.tanh(inside))

def gelu_slope(source):
    inside = root_coef * (source + cubic_coef * source * source * source)
    tanh_val = jnp.tanh(inside)
    return 0.5 * (1.0 + tanh_val) + 0.5 * source * (1.0 - tanh_val * tanh_val) * root_coef * (1.0 + 3.0 * cubic_coef * source * source)

def smooth_slope(source):
    return source / jnp.sqrt(source * source + smooth * smooth)

def stacked_taps(padded, row_count, col_count, flipped):
    pieces = []
    for row_tap in range(3):
        for col_tap in range(3):
            row_at = 2 - row_tap if flipped else row_tap
            col_at = 2 - col_tap if flipped else col_tap
            pieces.append(padded[:, row_at:row_at + row_count, col_at:col_at + col_count])
    return jnp.concatenate(pieces, axis=0).reshape(9 * padded.shape[0], row_count * col_count)

def conv_apply(source, weight, flipped):
    row_count, col_count = (source.shape[1], source.shape[2])
    padded = jnp.pad(source, ((0, 0), (1, 1), (1, 1)))
    if flipped:
        matrix = jnp.transpose(weight, (3, 0, 1, 2)).reshape(weight.shape[3], -1)
    else:
        matrix = jnp.transpose(weight, (2, 0, 1, 3)).reshape(weight.shape[2], -1)
    result = jnp.dot(matrix, stacked_taps(padded, row_count, col_count, flipped), preferred_element_type=jnp.float32)
    return result.reshape(matrix.shape[0], row_count, col_count)

def reference(features, skip, conv_weight, out_weight, target):
    member_total = features.shape[0]

    def forward_one(packed):
        source, bypass = packed
        preact = conv_apply(source, conv_weight, False) + bypass.astype(jnp.float32)
        active = gelu_value(preact).astype(jnp.bfloat16)
        flat = jnp.dot(out_weight, active.reshape(active.shape[0], -1), preferred_element_type=jnp.float32)
        return flat.reshape(out_weight.shape[0], active.shape[1], active.shape[2])
    outputs = lax.map(forward_one, (features, skip))

    def score_one(own_value):
        pair_term = lax.optimization_barrier(jnp.sum(smooth_slope(own_value[None] - outputs), axis=0))
        return smooth_slope(own_value - target) - pair_term / (member_total - 1)
    grad_out = lax.map(score_one, outputs).astype(jnp.bfloat16)

    def backward_one(triple):
        source, bypass, grad_member = triple
        preact = conv_apply(source, conv_weight, False) + bypass.astype(jnp.float32)
        flat = jnp.dot(out_weight.T, grad_member.reshape(grad_member.shape[0], -1), preferred_element_type=jnp.float32)
        grad_active = flat.reshape(preact.shape)
        grad_preact = (grad_active * gelu_slope(preact)).astype(jnp.bfloat16)
        return conv_apply(grad_preact, conv_weight, True).astype(jnp.bfloat16)
    return lax.map(backward_one, (features, skip, grad_out))
```

```python
import functools
import math

import jax
import jax.numpy as jnp
from jax import lax
from jax.experimental import pallas as pl
from jax.experimental.pallas import tpu as pltpu
from jax.sharding import PartitionSpec as P

root_coef = math.sqrt(2.0 / math.pi)
cubic_coef = 0.044715
smooth = 0.25
lane = 128
MESH = pl.DeviceIdType.MESH
F32 = jnp.float32
BF16 = jnp.bfloat16


def gelu_half(source, square):
    return 0.5 + 0.5 * jnp.tanh(source * (root_coef + (root_coef * cubic_coef) * square))


def gelu_value(source):
    return source * gelu_half(source, source * source)


def gelu_slope(source):
    square = source * source
    half = gelu_half(source, square)
    rate = 2.0 * root_coef + (6.0 * root_coef * cubic_coef) * square
    return half + (source * half) * ((1.0 - half) * rate)


def smooth_slope(source):
    return source * lax.rsqrt(source * source + smooth * smooth)


def dot(left, right):
    return lax.dot_general(left, right, (((1,), (0,)), ((), ())), preferred_element_type=F32)


def dot_nt(left, right):
    return lax.dot_general(left, right, (((1,), (1,)), ((), ())), preferred_element_type=F32)


def split_index(shape, dim, size):
    index = lax.broadcasted_iota(jnp.int32, shape, dim)
    if size & (size - 1) == 0:
        return lax.shift_right_logical(index, size.bit_length() - 1), index & (size - 1)
    return lax.div(index, size), lax.rem(index, size)


def shifted(value, step):
    count = value.shape[1]
    edge = jnp.zeros((value.shape[0], 1), value.dtype)
    if step == 1:
        return jnp.concatenate([value[:, 1:], edge], axis=1)
    return jnp.concatenate([edge, value[:, : count - 1]], axis=1)


def kernel(
    dims, x_hbm, skip_hbm, weight_hbm, out_w_hbm, target_hbm, pre, hgk, wbh,
    x, skip, weight, out_w, target, hstk, act, slope, hs, hx, hse, hgo, outs, osend, ybuf,
    gout, gsend, se, wf, wfh, wb, band, wo, wcol, wrow, sel,
    in_sem, hs_sem, hx_sem, gs_sem, hg_sem, as_sem, ar_sem, cs_sem, cr_sem,
):
    members, chans, rows, cols, peers, count, outn, chunk = dims
    full = chans * rows
    me = lax.axis_index("member")
    at = lax.axis_index("space")
    has_up = at > 0
    has_dn = at < count - 1
    up = {"space": lax.max(at - 1, 0)}
    dn = {"space": lax.min(at + 1, count - 1)}

    loads = [pltpu.make_async_copy(x_hbm.at[m], x.at[m], in_sem.at[m]) for m in range(members)]
    skips = [
        pltpu.make_async_copy(skip_hbm.at[m], skip.at[m], in_sem.at[members + m])
        for m in range(members)
    ]
    tgt = pltpu.make_async_copy(target_hbm, target, in_sem.at[2 * members])
    taps = pltpu.make_async_copy(weight_hbm, weight, in_sem.at[2 * members + 1])
    heads = pltpu.make_async_copy(out_w_hbm, out_w, in_sem.at[2 * members + 2])
    for c in loads[:1] + [taps, heads] + loads[1:] + skips + [tgt]:
        c.start()

    barrier = pltpu.get_barrier_semaphore()
    for d in range(1, peers):
        pl.semaphore_signal(
            barrier, inc=1, device_id={"member": lax.rem(me + d, peers)}, device_id_type=MESH
        )

    @pl.when(has_up)
    def _():
        pl.semaphore_signal(barrier, inc=1, device_id=up, device_id_type=MESH)

    @pl.when(has_dn)
    def _():
        pl.semaphore_signal(barrier, inc=1, device_id=dn, device_id_type=MESH)

    chan, row = split_index((2 * chans, full), 1, rows)
    half, pick = split_index((2 * chans, full), 0, chans)
    sel[...] = (
        (chan == pick) & (row == jnp.where(half == 0, 0, rows - 1))
    ).astype(F32).astype(BF16)

    left_chan, left_row = split_index((full, chans), 0, rows)
    spread = (left_chan == lax.broadcasted_iota(jnp.int32, (full, chans), 1)).astype(F32)
    spread_first = jnp.where(left_row == 0, spread, 0.0).astype(BF16)
    spread_last = jnp.where(left_row == rows - 1, spread, 0.0).astype(BF16)
    spread = spread.astype(BF16)

    def build_forward():
        taps.wait()
        wide = dot_nt(weight[...].reshape(9 * chans, chans), spread)
        lane_row = lax.broadcasted_iota(jnp.int32, (chans, lane), 1) & (rows - 1)
        for dc in range(3):
            for tile in range(full // lane):
                cut = slice(tile * lane, (tile + 1) * lane)
                tap = [wide[(3 * dr + dc) * chans : (3 * dr + dc + 1) * chans, cut] for dr in range(3)]
                for r in range(rows):
                    line = jnp.where(lane_row == r, tap[1], 0.0)
                    if r > 0:
                        line = jnp.where(lane_row == r - 1, tap[0], line)
                    if r < rows - 1:
                        line = jnp.where(lane_row == r + 1, tap[2], line)
                    band[dc, tile, pl.ds(r, chans, stride=rows), :] = line
                wf[:, dc * full + tile * lane : dc * full + (tile + 1) * lane] = band[
                    dc, tile
                ].astype(BF16)

    def build_edges(halo, flipped):
        pieces = []
        for dc in range(3):
            for dr in (2, 0) if flipped else (0, 2):
                tap = weight[dr, dc].astype(F32)
                pieces.append(tap.T if flipped else tap)
        line = jnp.concatenate(pieces, axis=1)
        slot, _ = split_index((chans, 6 * chans), 1, chans)
        first = jnp.where(slot & 1 == 0, line, 0.0).astype(BF16)
        last = jnp.where(slot & 1 == 1, line, 0.0).astype(BF16)
        halo[...] = dot(spread_first, first).astype(BF16) + dot(spread_last, last).astype(BF16)

    def build_backward():
        for dc in range(3):
            span = slice(dc * full, (dc + 1) * full)
            wb[:, span] = wf[:, span].T

    for absent, side in ((jnp.logical_not(has_up), 0), (jnp.logical_not(has_dn), 1)):

        @pl.when(absent)
        def _(side=side):
            for landing in (hx, hse, hgo):
                for m in range(members):
                    landing[m, side] = jnp.zeros(landing.shape[2:], landing.dtype)

    pl.semaphore_wait(
        barrier, peers - 1 + has_up.astype(jnp.int32) + has_dn.astype(jnp.int32)
    )

    def edge_of(src, m, half):
        return src.at[m, half] if len(src.shape) == 4 else src.at[m]

    def halo_copies(m, src, dst, send, recv):
        to_up = pltpu.make_async_remote_copy(
            src_ref=edge_of(src, m, 0), dst_ref=dst.at[m, 1], send_sem=send.at[m, 0],
            recv_sem=recv.at[m, 1], device_id=up, device_id_type=MESH,
        )
        to_dn = pltpu.make_async_remote_copy(
            src_ref=edge_of(src, m, 1), dst_ref=dst.at[m, 0], send_sem=send.at[m, 1],
            recv_sem=recv.at[m, 0], device_id=dn, device_id_type=MESH,
        )
        return to_up, to_dn

    def halo_start(which, src, dst, send, recv):
        copies = [halo_copies(m, src, dst, send, recv) for m in which]

        @pl.when(has_up)
        def _():
            for to_up, _ in copies:
                to_up.start()

        @pl.when(has_dn)
        def _():
            for _, to_dn in copies:
                to_dn.start()

    def halo_wait(which, exchanges, kind):
        copies = [halo_copies(m, *exchange) for exchange in exchanges for m in which]

        @pl.when(has_up)
        def _():
            for to_up, to_dn in copies:
                to_up.wait_send() if kind == "send" else to_dn.wait_recv()

        @pl.when(has_dn)
        def _():
            for to_up, to_dn in copies:
                to_dn.wait_send() if kind == "send" else to_up.wait_recv()

    def send_edges(m, source, store, dst, send, recv):
        edge = dot(sel[...], source).astype(BF16)
        store[m, 0] = edge[:chans]
        store[m, 1] = edge[chans:]
        halo_start((m,), store, dst, send, recv)

    def stack_halo(m, above, below, into, order):
        both = jnp.concatenate([above, below], axis=0)
        for slot, step in enumerate(order):
            value = both if step == 0 else shifted(both, step)
            into[m, slot * 2 * chans : (slot + 1) * 2 * chans, :] = value

    def widened(src, m, order):
        value = src[m]
        return [value if step == 0 else shifted(value, step) for step in order]

    def convolve(taps, wide, span):
        return dot(taps[...], jnp.concatenate([value[:, span] for value in wide], axis=0))

    spans = [slice(n, n + chunk) for n in range(0, cols, chunk)]

    def get(m, span, lines=slice(None)):
        tiles = range(span.start // lane, span.stop // lane)
        return jnp.concatenate([pre[m, tile, lines, :] for tile in tiles], axis=1)

    def put(m, span, value, lines=slice(None)):
        for k, tile in enumerate(range(span.start // lane, span.stop // lane)):
            pre[m, tile, lines, :] = value[:, k * lane : (k + 1) * lane]

    for m in range(members):
        loads[m].wait()
        send_edges(m, x[m], hs, hx, hs_sem, hx_sem)
    build_forward()
    build_edges(wfh, False)
    heads.wait()

    out_k, _ = split_index((outn * rows, chans), 0, rows)
    lines = jnp.zeros((outn * rows, chans), F32)
    for k in range(outn):
        lines = jnp.where(out_k == k, out_w[k : k + 1, :].astype(F32), lines)
    lines = lines.astype(BF16)
    _, oa = split_index((outn * rows, full), 0, rows)
    _, ob = split_index((outn * rows, full), 1, rows)
    wo[...] = jnp.where(oa == ob, dot_nt(lines, spread), 0.0).astype(BF16)
    for m in range(members):
        skips[m].wait()
    for m in range(members):
        wide = widened(x, m, (-1, 0, 1))
        for span in spans:
            put(m, span, convolve(wf, wide, span) + skip[m, :, span].astype(F32))

    parts = [slice(n, n + cols // 2) for n in range(0, cols, cols // 2)]

    def gather_copy(m, part, d):
        return pltpu.make_async_remote_copy(
            src_ref=osend.at[m, :, parts[part]],
            dst_ref=ybuf.at[d, m, :, parts[part]],
            send_sem=as_sem.at[m, part, d], recv_sem=ar_sem.at[m, part, d],
            device_id={"member": lax.rem(me + d, peers)}, device_id_type=MESH,
        )

    def project(m, part):
        for n in range(parts[part].start, parts[part].stop, chunk):
            span = slice(n, n + chunk)
            value = dot(wo[...], act[m, :, span])
            outs[m, :, span] = value
            osend[m, :, span] = value.astype(BF16)
        for d in range(1, peers):
            gather_copy(m, part, d).start()

    waiting = None
    for m in range(members):
        halo_wait((m,), [(hs, hx, hs_sem, hx_sem)], "recv")
        stack_halo(m, hx[m, 0], hx[m, 1], hstk, (-1, 0, 1))
        for part, range_of in enumerate(parts):
            for n in range(range_of.start, range_of.stop, chunk):
                span = slice(n, n + chunk)
                total = get(m, span) + dot(wfh[...], hstk[m, :, span])
                put(m, span, total)
                act[m, :, span] = gelu_value(total).astype(BF16)
            if waiting is not None:
                project(*waiting)
            waiting = (m, part)
    project(*waiting)

    block = 8 * rows
    for m in range(members):
        for n in range(0, full, block):
            for span in spans:
                lines = slice(n, n + block)
                slope[m, lines, span] = gelu_slope(get(m, span, lines)).astype(BF16)
        send_edges(m, slope[m], se, hse, gs_sem, hg_sem)
    build_backward()
    build_edges(wbh, True)
    eye = (
        lax.broadcasted_iota(jnp.int32, (chans, chans), 0)
        == lax.broadcasted_iota(jnp.int32, (chans, chans), 1)
    ).astype(F32).astype(BF16)
    for k in range(outn):
        flat = jnp.broadcast_to(out_w[k : k + 1, :].astype(F32), (chunk, chans)).astype(BF16)
        wcol[k] = dot_nt(spread, flat).astype(BF16)
        wrow[k] = dot_nt(eye, flat[:lane])

    tgt.wait()
    total_members = peers * members
    for part in range(2):
        for d in range(1, peers):
            for m in range(members):
                gather_copy(m, part, d).wait_recv()
        for n in range(parts[part].start, parts[part].stop, chunk):
            span = slice(n, n + chunk)
            own = [outs[m, :, span] for m in range(members)]
            pairs = [smooth_slope(v - v) for v in own]
            for i in range(members):
                for j in range(i):
                    term = smooth_slope(own[i] - own[j])
                    pairs[i] = pairs[i] + term
                    pairs[j] = pairs[j] - term
            for d in range(1, peers):
                for j in range(members):
                    other = ybuf[d, j, :, span].astype(F32)
                    for i in range(members):
                        pairs[i] = pairs[i] + smooth_slope(own[i] - other)
            for i in range(members):
                grad = smooth_slope(own[i] - target[:, span]) - pairs[i] / (total_members - 1)
                for k in range(outn):
                    part_k = grad[k * rows : (k + 1) * rows]
                    gout[i, k, :, span] = part_k.astype(BF16)
                    gsend[i, 0, k : k + 1, span] = part_k[:1]
                    gsend[i, 1, k : k + 1, span] = part_k[rows - 1 :]

    halo_start(range(members), gsend, hgo, cs_sem, cr_sem)
    def activate(m, span):
        for n in range(0, full, rows):
            lines = slice(n, n + rows)
            grad = wcol[0, lines, :] * gout[m, 0, :, span]
            for k in range(1, outn):
                grad = grad + wcol[k, lines, :] * gout[m, k, :, span]
            act[m, lines, span] = grad * slope[m, lines, span]

    for m in range(members):
        for span in spans:
            activate(m, span)
        wide = widened(act, m, (1, 0, -1))
        for span in spans:
            put(m, span, convolve(wb, wide, span))
    halo_wait(range(members), [(se, hse, gs_sem, hg_sem), (gsend, hgo, cs_sem, cr_sem)], "recv")
    for m in range(members):
        both = []
        for half in range(2):
            tiles = []
            for c in range(0, cols, lane):
                span = slice(c, c + lane)
                grad = wrow[0] * hgo[m, half, 0:1, span].astype(BF16).astype(F32)
                for k in range(1, outn):
                    grad = grad + wrow[k] * hgo[m, half, k : k + 1, span].astype(BF16).astype(F32)
                tiles.append((grad * hse[m, half, :, span].astype(F32)).astype(BF16))
            both.append(jnp.concatenate(tiles, axis=1))
        stack_halo(m, both[0], both[1], hgk, (1, 0, -1))

    halo_wait(
        range(members),
        [(hs, hx, hs_sem, hx_sem), (se, hse, gs_sem, hg_sem), (gsend, hgo, cs_sem, cr_sem)],
        "send",
    )
    for m in range(members):
        for part in range(2):
            for d in range(1, peers):
                gather_copy(m, part, d).wait_send()


def finish(dims, pre, hgk, wbh, out_hbm, out, sem):
    members, cols, chunk = dims
    copies = []
    for m in range(members):
        for n in range(0, cols, chunk):
            span = slice(n, n + chunk)
            main = jnp.concatenate([pre[m, (n + k) // lane] for k in range(0, chunk, lane)], axis=1)
            out[m, :, span] = (main + dot(wbh[...], hgk[m, :, span])).astype(BF16)
            copy = pltpu.make_async_copy(
                out.at[m, :, span], out_hbm.at[m, :, span], sem.at[m, n // chunk]
            )
            copy.start()
            copies.append(copy)
    for copy in copies:
        copy.wait()


def local(features, skip, conv_weight, out_weight, target):
    members, chans, rows, cols = features.shape
    outn = out_weight.shape[0]
    peers = lax.axis_size("member")
    count = lax.axis_size("space")
    full = chans * rows
    chunk = min(cols, 256)
    dims = (members, chans, rows, cols, peers, count, outn, chunk)
    dma = pltpu.SemaphoreType.DMA
    anywhere = pl.BlockSpec(memory_space=pltpu.HBM)
    vmem = pl.BlockSpec(memory_space=pltpu.VMEM)
    outer = (
        pltpu.VMEM((members, cols // lane, full, lane), F32),
        pltpu.VMEM((members, 6 * chans, cols), BF16),
        pltpu.VMEM((full, 6 * chans), BF16),
    )
    held = pl.pallas_call(
        functools.partial(kernel, dims),
        out_shape=outer,
        in_specs=[anywhere] * 5,
        out_specs=(vmem, vmem, vmem),
        scratch_shapes=[
            pltpu.VMEM((members, full, cols), BF16),
            pltpu.VMEM((members, full, cols), BF16),
            pltpu.VMEM(conv_weight.shape, BF16),
            pltpu.VMEM(out_weight.shape, BF16),
            pltpu.VMEM((outn * rows, cols), F32),
            pltpu.VMEM((members, 6 * chans, cols), BF16),
            pltpu.VMEM((members, full, cols), BF16),
            pltpu.VMEM((members, full, cols), BF16),
            pltpu.VMEM((members, 2, chans, cols), BF16),
            pltpu.VMEM((members, 2, chans, cols), BF16),
            pltpu.VMEM((members, 2, chans, cols), BF16),
            pltpu.VMEM((members, 2, outn, cols), F32),
            pltpu.VMEM((members, outn * rows, cols), F32),
            pltpu.VMEM((members, outn * rows, cols), BF16),
            pltpu.VMEM((peers, members, outn * rows, cols), BF16),
            pltpu.VMEM((members, outn, rows, cols), BF16),
            pltpu.VMEM((members, 2, outn, cols), F32),
            pltpu.VMEM((members, 2, chans, cols), BF16),
            pltpu.VMEM((full, 3 * full), BF16),
            pltpu.VMEM((full, 6 * chans), BF16),
            pltpu.VMEM((full, 3 * full), BF16),
            pltpu.VMEM((3, full // lane, full, lane), F32),
            pltpu.VMEM((outn * rows, full), BF16),
            pltpu.VMEM((outn, full, chunk), BF16),
            pltpu.VMEM((outn, chans, lane), F32),
            pltpu.VMEM((2 * chans, full), BF16),
            dma((2 * members + 3,)),
            dma((members, 2)),
            dma((members, 2)),
            dma((members, 2)),
            dma((members, 2)),
            dma((members, 2, peers)),
            dma((members, 2, peers)),
            dma((members, 2)),
            dma((members, 2)),
        ],
        compiler_params=pltpu.CompilerParams(collective_id=0, has_side_effects=True, vmem_limit_bytes=58 * 2**20),
    )(
        features.reshape(members, full, cols),
        skip.reshape(members, full, cols),
        conv_weight,
        out_weight,
        target.reshape(outn * rows, cols),
    )
    result = pl.pallas_call(
        functools.partial(finish, (members, cols, chunk)),
        out_shape=jax.ShapeDtypeStruct((members, full, cols), BF16),
        in_specs=[vmem, vmem, vmem],
        out_specs=anywhere,
        scratch_shapes=[pltpu.VMEM((members, full, cols), BF16), dma((members, cols // chunk))],
        compiler_params=pltpu.CompilerParams(vmem_limit_bytes=16 * 2**20),
    )(*held)
    return result.reshape(members, chans, rows, cols)


def solution(mesh):
    placed = (
        P("member", None, "space", None),
        P("member", None, "space", None),
        P(),
        P(),
        P(None, "space", None),
    )
    return jax.shard_map(
        local,
        mesh=mesh,
        in_specs=placed,
        out_specs=P("member", None, "space", None),
        check_vma=False,
    )
```

```python
import functools
import math

import jax
import jax.numpy as jnp
from jax import lax
from jax.experimental import pallas as pl
from jax.experimental.pallas import tpu as pltpu
from jax.sharding import PartitionSpec as P

root_coef = math.sqrt(2.0 / math.pi)
cubic_coef = 0.044715
smooth = 0.25
lane = 128
MESH = pl.DeviceIdType.MESH
F32 = jnp.float32
BF16 = jnp.bfloat16


def gelu_half(source, square):
    return 0.5 + 0.5 * jnp.tanh(source * (root_coef + (root_coef * cubic_coef) * square))


def gelu_value(source):
    return source * gelu_half(source, source * source)


def gelu_slope(source):
    square = source * source
    half = gelu_half(source, square)
    rate = 2.0 * root_coef + (6.0 * root_coef * cubic_coef) * square
    return half + (source * half) * ((1.0 - half) * rate)


def smooth_slope(source):
    return source * lax.rsqrt(source * source + smooth * smooth)


def dot(left, right):
    return lax.dot_general(left, right, (((1,), (0,)), ((), ())), preferred_element_type=F32)


def dot_nt(left, right):
    return lax.dot_general(left, right, (((1,), (1,)), ((), ())), preferred_element_type=F32)


def split_index(shape, dim, size):
    index = lax.broadcasted_iota(jnp.int32, shape, dim)
    if size & (size - 1) == 0:
        return lax.shift_right_logical(index, size.bit_length() - 1), index & (size - 1)
    return lax.div(index, size), lax.rem(index, size)


def shifted(value, step):
    count = value.shape[1]
    edge = jnp.zeros((value.shape[0], 1), value.dtype)
    if step == 1:
        return jnp.concatenate([value[:, 1:], edge], axis=1)
    return jnp.concatenate([edge, value[:, : count - 1]], axis=1)


def kernel(
    dims, x_hbm, skip_hbm, weight_hbm, out_w_hbm, target_hbm, pre,
    x, skip, weight, out_w, target, hstk, act, slope, hs, hx, hse, hgo, outs, osend, ybuf, esend, yedge,
    gout, gsend, se, wf, wfh, wb, wbh, band, wo, woe, wcol, wrow, sel,
    in_sem, hs_sem, hx_sem, gs_sem, hg_sem, as_sem, ar_sem, es_sem, er_sem, cs_sem, cr_sem,
):
    members, chans, rows, cols, peers, count, outn, chunk = dims
    full = chans * rows
    me = lax.axis_index("member")
    at = lax.axis_index("space")
    has_up = at > 0
    has_dn = at < count - 1
    up = {"space": lax.max(at - 1, 0)}
    dn = {"space": lax.min(at + 1, count - 1)}

    loads = [pltpu.make_async_copy(x_hbm.at[m], x.at[m], in_sem.at[m]) for m in range(members)]
    skips = [
        pltpu.make_async_copy(skip_hbm.at[m], skip.at[m], in_sem.at[members + m])
        for m in range(members)
    ]
    tgt = pltpu.make_async_copy(target_hbm, target, in_sem.at[2 * members])
    taps = pltpu.make_async_copy(weight_hbm, weight, in_sem.at[2 * members + 1])
    heads = pltpu.make_async_copy(out_w_hbm, out_w, in_sem.at[2 * members + 2])
    for c in loads[:1] + [taps, heads] + loads[1:] + skips + [tgt]:
        c.start()

    barrier = pltpu.get_barrier_semaphore()
    for d in range(1, peers):
        pl.semaphore_signal(
            barrier, inc=1, device_id={"member": lax.rem(me + d, peers)}, device_id_type=MESH
        )

    @pl.when(has_up)
    def _():
        pl.semaphore_signal(barrier, inc=1, device_id=up, device_id_type=MESH)

    @pl.when(has_dn)
    def _():
        pl.semaphore_signal(barrier, inc=1, device_id=dn, device_id_type=MESH)

    chan, row = split_index((2 * chans, full), 1, rows)
    half, pick = split_index((2 * chans, full), 0, chans)
    sel[...] = (
        (chan == pick) & (row == jnp.where(half == 0, 0, rows - 1))
    ).astype(F32).astype(BF16)

    left_chan, _ = split_index((full, chans), 0, rows)
    spread = (left_chan == lax.broadcasted_iota(jnp.int32, (full, chans), 1)).astype(F32)
    spread = spread.astype(BF16)

    def build_forward():
        taps.wait()
        wide = dot_nt(weight[...].reshape(9 * chans, chans), spread)
        lane_row = lax.broadcasted_iota(jnp.int32, (chans, lane), 1) & (rows - 1)
        for dc in range(3):
            for tile in range(full // lane):
                cut = slice(tile * lane, (tile + 1) * lane)
                tap = [wide[(3 * dr + dc) * chans : (3 * dr + dc + 1) * chans, cut] for dr in range(3)]
                for r in range(rows):
                    line = jnp.where(lane_row == r, tap[1], 0.0)
                    if r > 0:
                        line = jnp.where(lane_row == r - 1, tap[0], line)
                    if r < rows - 1:
                        line = jnp.where(lane_row == r + 1, tap[2], line)
                    band[dc, tile, pl.ds(r, chans, stride=rows), :] = line
                wf[:, dc * full + tile * lane : dc * full + (tile + 1) * lane] = band[
                    dc, tile
                ].astype(BF16)

    def build_edges(halo, flipped):
        pieces = []
        for dc in range(3):
            for dr in (2, 0) if flipped else (0, 2):
                tap = weight[dr, dc].astype(F32)
                pieces.append(tap.T if flipped else tap)
        line = jnp.concatenate(pieces, axis=1)
        slot, _ = split_index((chans, 6 * chans), 1, chans)
        first = jnp.where(slot & 1 == 0, line, 0.0).astype(BF16)
        last = jnp.where(slot & 1 == 1, line, 0.0).astype(BF16)
        halo[...] = jnp.concatenate([first, last], axis=0)

    def build_backward():
        for dc in range(3):
            span = slice(dc * full, (dc + 1) * full)
            wb[:, span] = wf[:, span].T

    for absent, side in ((jnp.logical_not(has_up), 0), (jnp.logical_not(has_dn), 1)):

        @pl.when(absent)
        def _(side=side):
            for landing in (hx, hse, hgo):
                for m in range(members):
                    landing[m, side] = jnp.zeros(landing.shape[2:], landing.dtype)

    pl.semaphore_wait(
        barrier, peers - 1 + has_up.astype(jnp.int32) + has_dn.astype(jnp.int32)
    )

    def edge_of(src, m, half):
        return src.at[m, half] if len(src.shape) == 4 else src.at[m]

    def halo_copies(m, src, dst, send, recv):
        to_up = pltpu.make_async_remote_copy(
            src_ref=edge_of(src, m, 0), dst_ref=dst.at[m, 1], send_sem=send.at[m, 0],
            recv_sem=recv.at[m, 1], device_id=up, device_id_type=MESH,
        )
        to_dn = pltpu.make_async_remote_copy(
            src_ref=edge_of(src, m, 1), dst_ref=dst.at[m, 0], send_sem=send.at[m, 1],
            recv_sem=recv.at[m, 0], device_id=dn, device_id_type=MESH,
        )
        return to_up, to_dn

    def halo_start(which, src, dst, send, recv):
        copies = [halo_copies(m, src, dst, send, recv) for m in which]

        @pl.when(has_up)
        def _():
            for to_up, _ in copies:
                to_up.start()

        @pl.when(has_dn)
        def _():
            for _, to_dn in copies:
                to_dn.start()

    def halo_wait(which, exchanges, kind):
        copies = [halo_copies(m, *exchange) for exchange in exchanges for m in which]

        @pl.when(has_up)
        def _():
            for to_up, to_dn in copies:
                to_up.wait_send() if kind == "send" else to_dn.wait_recv()

        @pl.when(has_dn)
        def _():
            for to_up, to_dn in copies:
                to_dn.wait_send() if kind == "send" else to_up.wait_recv()

    def send_edges(m, source, store, dst, send, recv):
        edge = dot(sel[...], source).astype(BF16)
        store[m, 0] = edge[:chans]
        store[m, 1] = edge[chans:]
        halo_start((m,), store, dst, send, recv)

    def stack_halo(m, above, below, into, order):
        both = jnp.concatenate([above, below], axis=0)
        for slot, step in enumerate(order):
            value = both if step == 0 else shifted(both, step)
            into[m, slot * 2 * chans : (slot + 1) * 2 * chans, :] = value

    def widened(src, m, order):
        value = src[m]
        return [value if step == 0 else shifted(value, step) for step in order]

    def convolve(taps, wide, span):
        return dot(taps[...], jnp.concatenate([value[:, span] for value in wide], axis=0))

    def edge_rows(m, span):
        tiles = range(span.start // lane, span.stop // lane)
        halves = [
            jnp.concatenate(
                [pre[m, t, pl.ds(side * (rows - 1), chans, stride=rows), :] for t in tiles], axis=1
            )
            for side in range(2)
        ]
        return jnp.concatenate(halves, axis=0)

    def put_edge_rows(m, span, value):
        for side in range(2):
            for k, t in enumerate(range(span.start // lane, span.stop // lane)):
                pre[m, t, pl.ds(side * (rows - 1), chans, stride=rows), :] = value[
                    side * chans : (side + 1) * chans, k * lane : (k + 1) * lane
                ]

    spans = [slice(n, n + chunk) for n in range(0, cols, chunk)]

    def get(m, span, lines=slice(None)):
        tiles = range(span.start // lane, span.stop // lane)
        return jnp.concatenate([pre[m, tile, lines, :] for tile in tiles], axis=1)

    def put(m, span, value, lines=slice(None)):
        for k, tile in enumerate(range(span.start // lane, span.stop // lane)):
            pre[m, tile, lines, :] = value[:, k * lane : (k + 1) * lane]

    for m in range(members):
        loads[m].wait()
        send_edges(m, x[m], hs, hx, hs_sem, hx_sem)
    build_forward()
    build_edges(wfh, False)
    heads.wait()

    out_k, _ = split_index((outn * rows, chans), 0, rows)
    lines = jnp.zeros((outn * rows, chans), F32)
    for k in range(outn):
        lines = jnp.where(out_k == k, out_w[k : k + 1, :].astype(F32), lines)
    lines = lines.astype(BF16)
    _, oa = split_index((outn * rows, full), 0, rows)
    _, ob = split_index((outn * rows, full), 1, rows)
    wo[...] = jnp.where(oa == ob, dot_nt(lines, spread), 0.0).astype(BF16)
    shape = (2 * outn, 2 * chans)
    edge_k, edge_side = split_index(shape, 0, 2)
    edge_half, _ = split_index(shape, 1, chans)
    twice = jnp.concatenate([out_w[...].astype(F32)] * 2, axis=1)
    lines = jnp.zeros(shape, F32)
    for k in range(outn):
        lines = jnp.where(edge_k == k, twice[k : k + 1], lines)
    woe[...] = jnp.where(edge_side == edge_half, lines, 0.0).astype(BF16)
    for m in range(members):
        skips[m].wait()
    parts = [slice(n, n + cols // 2) for n in range(0, cols, cols // 2)]

    def partner(d):
        if peers & (peers - 1):
            return lax.rem(me + d, peers)
        flipped, bit = 0, 1
        while bit < peers:
            flipped = flipped + bit * lax.rem(lax.div(me, bit) + (d // bit) % 2, 2)
            bit *= 2
        return flipped

    def edge_copy(m, d):
        return pltpu.make_async_remote_copy(
            src_ref=esend.at[m], dst_ref=yedge.at[d, m],
            send_sem=es_sem.at[m, d], recv_sem=er_sem.at[m, d],
            device_id={"member": partner(d)}, device_id_type=MESH,
        )

    others = range(peers - 1, 0, -1)

    def gather_copy(m, part, d):
        return pltpu.make_async_remote_copy(
            src_ref=osend.at[m, :, parts[part]],
            dst_ref=ybuf.at[d, m, :, parts[part]],
            send_sem=as_sem.at[m, part, d], recv_sem=ar_sem.at[m, part, d],
            device_id={"member": partner(d)}, device_id_type=MESH,
        )

    def project(m, part, values):
        for n, value in values:
            span = slice(n, n + chunk)
            value = dot(wo[...], value)
            outs[m, :, span] = value
            osend[m, :, span] = value.astype(BF16)
        for d in others:
            gather_copy(m, part, d).start()

    waiting = None
    for m in range(members):
        wide = widened(x, m, (-1, 0, 1))
        for part, range_of in enumerate(parts):
            values = []
            for n in range(range_of.start, range_of.stop, chunk):
                span = slice(n, n + chunk)
                total = convolve(wf, wide, span) + skip[m, :, span].astype(F32)
                put(m, span, total)
                values.append((n, gelu_value(total).astype(BF16)))
            if waiting is not None:
                project(*waiting)
            waiting = (m, part, values)
    project(*waiting)

    for m in range(members):
        halo_wait((m,), [(hs, hx, hs_sem, hx_sem)], "recv")
        stack_halo(m, hx[m, 0], hx[m, 1], hstk, (-1, 0, 1))
        for span in spans:
            total = edge_rows(m, span) + dot(wfh[...], hstk[m, :, span])
            put_edge_rows(m, span, total)
            value = dot(woe[...], gelu_value(total).astype(BF16))
            esend[m, :, span] = value.astype(BF16)
            for k in range(outn):
                for side in range(2):
                    row = k * rows + side * (rows - 1)
                    outs[m, row : row + 1, span] = value[2 * k + side : 2 * k + side + 1]
        for d in others:
            edge_copy(m, d).start()

    block = 8 * rows
    for m in range(members):
        for n in range(0, full, block):
            for span in spans:
                lines = slice(n, n + block)
                slope[m, lines, span] = gelu_slope(get(m, span, lines)).astype(BF16)
        send_edges(m, slope[m], se, hse, gs_sem, hg_sem)
    build_backward()
    build_edges(wbh, True)
    eye = (
        lax.broadcasted_iota(jnp.int32, (chans, chans), 0)
        == lax.broadcasted_iota(jnp.int32, (chans, chans), 1)
    ).astype(F32).astype(BF16)
    for k in range(outn):
        flat = jnp.broadcast_to(out_w[k : k + 1, :].astype(F32), (chunk, chans)).astype(BF16)
        wcol[k] = dot_nt(spread, flat).astype(BF16)
        wrow[k] = dot_nt(eye, flat[:lane])

    tgt.wait()
    total_members = peers * members
    shape = (outn * rows, 2 * outn)
    out_k, out_r = split_index(shape, 0, rows)
    edge_k, edge_side = split_index(shape, 1, 2)
    widen = (
        (out_k == edge_k) & (out_r == jnp.where(edge_side == 0, 0, rows - 1))
    ).astype(F32).astype(BF16)
    _, out_r = split_index((outn * rows, chunk), 0, rows)
    at_edge = (out_r == 0) | (out_r == rows - 1)
    for m in range(members):
        for d in others:
            edge_copy(m, d).wait_recv()
    for part in range(2):
        for d in range(1, peers):
            for m in range(members):
                gather_copy(m, part, d).wait_recv()
        for n in range(parts[part].start, parts[part].stop, chunk):
            span = slice(n, n + chunk)
            own = [outs[m, :, span] for m in range(members)]
            pairs = [smooth_slope(v - v) for v in own]
            for i in range(members):
                for j in range(i):
                    term = smooth_slope(own[i] - own[j])
                    pairs[i] = pairs[i] + term
                    pairs[j] = pairs[j] - term
            for d in range(1, peers):
                for j in range(members):
                    other = jnp.where(
                        at_edge, dot(widen, yedge[d, j, :, span]), ybuf[d, j, :, span].astype(F32)
                    )
                    for i in range(members):
                        pairs[i] = pairs[i] + smooth_slope(own[i] - other)
            for i in range(members):
                grad = smooth_slope(own[i] - target[:, span]) - pairs[i] / (total_members - 1)
                for k in range(outn):
                    part_k = grad[k * rows : (k + 1) * rows]
                    gout[i, k, :, span] = part_k.astype(BF16)
                    gsend[i, 0, k : k + 1, span] = part_k[:1]
                    gsend[i, 1, k : k + 1, span] = part_k[rows - 1 :]

    halo_start(range(members), gsend, hgo, cs_sem, cr_sem)
    def activate(m, span):
        for n in range(0, full, rows):
            lines = slice(n, n + rows)
            grad = wcol[0, lines, :] * gout[m, 0, :, span]
            for k in range(1, outn):
                grad = grad + wcol[k, lines, :] * gout[m, k, :, span]
            act[m, lines, span] = grad * slope[m, lines, span]

    for m in range(members):
        for span in spans:
            activate(m, span)
        wide = widened(act, m, (1, 0, -1))
        for span in spans:
            put(m, span, convolve(wb, wide, span))
    halo_wait(range(members), [(se, hse, gs_sem, hg_sem), (gsend, hgo, cs_sem, cr_sem)], "recv")
    for m in range(members):
        both = []
        for half in range(2):
            tiles = []
            for c in range(0, cols, lane):
                span = slice(c, c + lane)
                grad = wrow[0] * hgo[m, half, 0:1, span].astype(BF16).astype(F32)
                for k in range(1, outn):
                    grad = grad + wrow[k] * hgo[m, half, k : k + 1, span].astype(BF16).astype(F32)
                tiles.append((grad * hse[m, half, :, span].astype(F32)).astype(BF16))
            both.append(jnp.concatenate(tiles, axis=1))
        stack_halo(m, both[0], both[1], hstk, (1, 0, -1))
        for span in spans:
            put_edge_rows(m, span, edge_rows(m, span) + dot(wbh[...], hstk[m, :, span]))

    halo_wait(
        range(members),
        [(hs, hx, hs_sem, hx_sem), (se, hse, gs_sem, hg_sem), (gsend, hgo, cs_sem, cr_sem)],
        "send",
    )
    for m in range(members):
        for part in range(2):
            for d in range(1, peers):
                gather_copy(m, part, d).wait_send()
        for d in others:
            edge_copy(m, d).wait_send()


def finish(dims, pre, out_hbm, out, sem):
    members, cols, chunk = dims
    copies = []
    for m in range(members):
        for n in range(0, cols, chunk):
            span = slice(n, n + chunk)
            tiles = [pre[m, (n + k) // lane] for k in range(0, chunk, lane)]
            out[m, :, span] = jnp.concatenate(tiles, axis=1).astype(BF16)
            copy = pltpu.make_async_copy(
                out.at[m, :, span], out_hbm.at[m, :, span], sem.at[m, n // chunk]
            )
            copy.start()
            copies.append(copy)
    for copy in copies:
        copy.wait()


def local(features, skip, conv_weight, out_weight, target):
    members, chans, rows, cols = features.shape
    outn = out_weight.shape[0]
    peers = lax.axis_size("member")
    count = lax.axis_size("space")
    full = chans * rows
    chunk = min(cols, 256)
    dims = (members, chans, rows, cols, peers, count, outn, chunk)
    dma = pltpu.SemaphoreType.DMA
    anywhere = pl.BlockSpec(memory_space=pltpu.HBM)
    vmem = pl.BlockSpec(memory_space=pltpu.VMEM)
    held = pl.pallas_call(
        functools.partial(kernel, dims),
        out_shape=pltpu.VMEM((members, cols // lane, full, lane), F32),
        in_specs=[anywhere] * 5,
        out_specs=vmem,
        scratch_shapes=[
            pltpu.VMEM((members, full, cols), BF16),
            pltpu.VMEM((members, full, cols), BF16),
            pltpu.VMEM(conv_weight.shape, BF16),
            pltpu.VMEM(out_weight.shape, BF16),
            pltpu.VMEM((outn * rows, cols), F32),
            pltpu.VMEM((members, 6 * chans, cols), BF16),
            pltpu.VMEM((members, full, cols), BF16),
            pltpu.VMEM((members, full, cols), BF16),
            pltpu.VMEM((members, 2, chans, cols), BF16),
            pltpu.VMEM((members, 2, chans, cols), BF16),
            pltpu.VMEM((members, 2, chans, cols), BF16),
            pltpu.VMEM((members, 2, outn, cols), F32),
            pltpu.VMEM((members, outn * rows, cols), F32),
            pltpu.VMEM((members, outn * rows, cols), BF16),
            pltpu.VMEM((peers, members, outn * rows, cols), BF16),
            pltpu.VMEM((members, 2 * outn, cols), BF16),
            pltpu.VMEM((peers, members, 2 * outn, cols), BF16),
            pltpu.VMEM((members, outn, rows, cols), BF16),
            pltpu.VMEM((members, 2, outn, cols), F32),
            pltpu.VMEM((members, 2, chans, cols), BF16),
            pltpu.VMEM((full, 3 * full), BF16),
            pltpu.VMEM((2 * chans, 6 * chans), BF16),
            pltpu.VMEM((full, 3 * full), BF16),
            pltpu.VMEM((2 * chans, 6 * chans), BF16),
            pltpu.VMEM((3, full // lane, full, lane), F32),
            pltpu.VMEM((outn * rows, full), BF16),
            pltpu.VMEM((2 * outn, 2 * chans), BF16),
            pltpu.VMEM((outn, full, chunk), BF16),
            pltpu.VMEM((outn, chans, lane), F32),
            pltpu.VMEM((2 * chans, full), BF16),
            dma((2 * members + 3,)),
            dma((members, 2)),
            dma((members, 2)),
            dma((members, 2)),
            dma((members, 2)),
            dma((members, 2, peers)),
            dma((members, 2, peers)),
            dma((members, peers)),
            dma((members, peers)),
            dma((members, 2)),
            dma((members, 2)),
        ],
        compiler_params=pltpu.CompilerParams(collective_id=0, has_side_effects=True, vmem_limit_bytes=58 * 2**20),
    )(
        features.reshape(members, full, cols),
        skip.reshape(members, full, cols),
        conv_weight,
        out_weight,
        target.reshape(outn * rows, cols),
    )
    result = pl.pallas_call(
        functools.partial(finish, (members, cols, chunk)),
        out_shape=jax.ShapeDtypeStruct((members, full, cols), BF16),
        in_specs=[vmem],
        out_specs=anywhere,
        scratch_shapes=[pltpu.VMEM((members, full, cols), BF16), dma((members, cols // chunk))],
        compiler_params=pltpu.CompilerParams(vmem_limit_bytes=16 * 2**20),
    )(held)
    return result.reshape(members, chans, rows, cols)


def solution(mesh):
    placed = (
        P("member", None, "space", None),
        P("member", None, "space", None),
        P(),
        P(),
        P(None, "space", None),
    )
    return jax.shard_map(
        local,
        mesh=mesh,
        in_specs=placed,
        out_specs=P("member", None, "space", None),
        check_vma=False,
    )
```

```python
import functools
import math

import jax
import jax.numpy as jnp
from jax import lax
from jax.experimental import pallas as pl
from jax.experimental.pallas import tpu as pltpu
from jax.sharding import PartitionSpec as P

root_coef = math.sqrt(2.0 / math.pi)
cubic_coef = 0.044715
smooth = 0.25
lane = 128
MESH = pl.DeviceIdType.MESH
F32 = jnp.float32
BF16 = jnp.bfloat16


def gelu_half(source, square):
    return 0.5 + 0.5 * jnp.tanh(source * (root_coef + (root_coef * cubic_coef) * square))


def gelu_value(source):
    return source * gelu_half(source, source * source)


def gelu_slope(source):
    square = source * source
    half = gelu_half(source, square)
    rate = 2.0 * root_coef + (6.0 * root_coef * cubic_coef) * square
    return half + (source * half) * ((1.0 - half) * rate)


def smooth_slope(source):
    return source * lax.rsqrt(source * source + smooth * smooth)


def dot(left, right):
    return lax.dot_general(left, right, (((1,), (0,)), ((), ())), preferred_element_type=F32)


def dot_nt(left, right):
    return lax.dot_general(left, right, (((1,), (1,)), ((), ())), preferred_element_type=F32)


def split_index(shape, dim, size):
    index = lax.broadcasted_iota(jnp.int32, shape, dim)
    if size & (size - 1) == 0:
        return lax.shift_right_logical(index, size.bit_length() - 1), index & (size - 1)
    return lax.div(index, size), lax.rem(index, size)


def shifted(value, step):
    count = value.shape[1]
    edge = jnp.zeros((value.shape[0], 1), value.dtype)
    if step == 1:
        return jnp.concatenate([value[:, 1:], edge], axis=1)
    return jnp.concatenate([edge, value[:, : count - 1]], axis=1)


def kernel(
    dims, x_hbm, skip_hbm, weight_hbm, out_w_hbm, target_hbm, pre,
    x, skip, weight, out_w, target, hstk, act, slope, hs, hx, hse, hgo, outs, osend, ybuf, esend, yedge, oute, tedge, pedge,
    gout, gsend, se, wf, wfh, wb, wbh, band, wo, woe, wcol, wrow, sel,
    in_sem, hs_sem, hx_sem, gs_sem, hg_sem, as_sem, ar_sem, es_sem, er_sem, cs_sem, cr_sem,
):
    members, chans, rows, cols, peers, count, outn, chunk = dims
    full = chans * rows
    me = lax.axis_index("member")
    at = lax.axis_index("space")
    has_up = at > 0
    has_dn = at < count - 1
    up = {"space": lax.max(at - 1, 0)}
    dn = {"space": lax.min(at + 1, count - 1)}

    loads = [pltpu.make_async_copy(x_hbm.at[m], x.at[m], in_sem.at[m]) for m in range(members)]
    skips = pltpu.make_async_copy(skip_hbm, skip, in_sem.at[members])
    tgt = pltpu.make_async_copy(target_hbm, target, in_sem.at[members + 1])
    taps = pltpu.make_async_copy(weight_hbm, weight, in_sem.at[members + 2])
    heads = pltpu.make_async_copy(out_w_hbm, out_w, in_sem.at[members + 3])
    for c in loads[:1] + [taps, heads] + loads[1:] + [skips, tgt]:
        c.start()

    barrier = pltpu.get_barrier_semaphore()
    for d in range(1, peers):
        pl.semaphore_signal(
            barrier, inc=1, device_id={"member": lax.rem(me + d, peers)}, device_id_type=MESH
        )

    @pl.when(has_up)
    def _():
        pl.semaphore_signal(barrier, inc=1, device_id=up, device_id_type=MESH)

    @pl.when(has_dn)
    def _():
        pl.semaphore_signal(barrier, inc=1, device_id=dn, device_id_type=MESH)

    chan, row = split_index((2 * chans, full), 1, rows)
    half, pick = split_index((2 * chans, full), 0, chans)
    sel[...] = (
        (chan == pick) & (row == jnp.where(half == 0, 0, rows - 1))
    ).astype(F32).astype(BF16)

    left_chan, _ = split_index((full, chans), 0, rows)
    spread = (left_chan == lax.broadcasted_iota(jnp.int32, (full, chans), 1)).astype(F32)
    spread = spread.astype(BF16)

    def build_forward():
        taps.wait()
        wide = dot_nt(weight[...].reshape(9 * chans, chans), spread)
        lane_row = lax.broadcasted_iota(jnp.int32, (chans, lane), 1) & (rows - 1)
        for dc in range(3):
            for tile in range(full // lane):
                cut = slice(tile * lane, (tile + 1) * lane)
                tap = [wide[(3 * dr + dc) * chans : (3 * dr + dc + 1) * chans, cut] for dr in range(3)]
                for r in range(rows):
                    line = jnp.where(lane_row == r, tap[1], 0.0)
                    if r > 0:
                        line = jnp.where(lane_row == r - 1, tap[0], line)
                    if r < rows - 1:
                        line = jnp.where(lane_row == r + 1, tap[2], line)
                    band[dc, tile, pl.ds(r, chans, stride=rows), :] = line
                wf[:, dc * full + tile * lane : dc * full + (tile + 1) * lane] = band[
                    dc, tile
                ].astype(BF16)

    def build_edges(halo, flipped):
        pieces = []
        for dc in range(3):
            for dr in (2, 0) if flipped else (0, 2):
                tap = weight[dr, dc].astype(F32)
                pieces.append(tap.T if flipped else tap)
        line = jnp.concatenate(pieces, axis=1)
        slot, _ = split_index((chans, 6 * chans), 1, chans)
        first = jnp.where(slot & 1 == 0, line, 0.0).astype(BF16)
        last = jnp.where(slot & 1 == 1, line, 0.0).astype(BF16)
        halo[...] = jnp.concatenate([first, last], axis=0)

    def build_backward():
        for dc in range(3):
            span = slice(dc * full, (dc + 1) * full)
            wb[:, span] = wf[:, span].T

    for absent, side in ((jnp.logical_not(has_up), 0), (jnp.logical_not(has_dn), 1)):

        @pl.when(absent)
        def _(side=side):
            for landing in (hx, hse, hgo):
                for m in range(members):
                    landing[side, m] = jnp.zeros(landing.shape[2:], landing.dtype)

    def halo_copies(src, dst, send, recv):
        to_up = pltpu.make_async_remote_copy(
            src_ref=src.at[0], dst_ref=dst.at[1], send_sem=send.at[0],
            recv_sem=recv.at[1], device_id=up, device_id_type=MESH,
        )
        to_dn = pltpu.make_async_remote_copy(
            src_ref=src.at[1], dst_ref=dst.at[0], send_sem=send.at[1],
            recv_sem=recv.at[0], device_id=dn, device_id_type=MESH,
        )
        return to_up, to_dn

    def halo_start(*exchange):
        to_up, to_dn = halo_copies(*exchange)

        @pl.when(has_up)
        def _():
            to_up.start()

        @pl.when(has_dn)
        def _():
            to_dn.start()

    def halo_wait(exchanges, kind):
        copies = [halo_copies(*exchange) for exchange in exchanges]

        @pl.when(has_up)
        def _():
            for to_up, to_dn in copies:
                to_up.wait_send() if kind == "send" else to_dn.wait_recv()

        @pl.when(has_dn)
        def _():
            for to_up, to_dn in copies:
                to_dn.wait_send() if kind == "send" else to_up.wait_recv()

    def extract_edges(m, source, store):
        edge = dot(sel[...], source).astype(BF16)
        store[0, m] = edge[:chans]
        store[1, m] = edge[chans:]

    def stack_halo(m, above, below, into, order):
        both = jnp.concatenate([above, below], axis=0)
        for slot, step in enumerate(order):
            value = both if step == 0 else shifted(both, step)
            into[m, slot * 2 * chans : (slot + 1) * 2 * chans, :] = value

    def widened(src, m, order):
        value = src[m]
        return [value if step == 0 else shifted(value, step) for step in order]

    def convolve(taps, wide, span):
        return dot(taps[...], jnp.concatenate([value[:, span] for value in wide], axis=0))

    def edge_rows(m, span):
        tiles = range(span.start // lane, span.stop // lane)
        halves = [
            jnp.concatenate(
                [pre[m, t, pl.ds(side * (rows - 1), chans, stride=rows), :] for t in tiles], axis=1
            )
            for side in range(2)
        ]
        return jnp.concatenate(halves, axis=0)

    def put_edge_rows(m, span, value):
        for side in range(2):
            for k, t in enumerate(range(span.start // lane, span.stop // lane)):
                pre[m, t, pl.ds(side * (rows - 1), chans, stride=rows), :] = value[
                    side * chans : (side + 1) * chans, k * lane : (k + 1) * lane
                ]

    spans = [slice(n, n + chunk) for n in range(0, cols, chunk)]

    def get(m, span, lines=slice(None)):
        tiles = range(span.start // lane, span.stop // lane)
        return jnp.concatenate([pre[m, tile, lines, :] for tile in tiles], axis=1)

    def put(m, span, value, lines=slice(None)):
        for k, tile in enumerate(range(span.start // lane, span.stop // lane)):
            pre[m, tile, lines, :] = value[:, k * lane : (k + 1) * lane]

    for m in range(members):
        loads[m].wait()
        extract_edges(m, x[m], hs)
    pl.semaphore_wait(
        barrier, peers - 1 + has_up.astype(jnp.int32) + has_dn.astype(jnp.int32)
    )
    halo_start(hs, hx, hs_sem, hx_sem)
    build_forward()
    build_edges(wfh, False)
    heads.wait()

    out_k, _ = split_index((outn * rows, chans), 0, rows)
    lines = jnp.zeros((outn * rows, chans), F32)
    for k in range(outn):
        lines = jnp.where(out_k == k, out_w[k : k + 1, :].astype(F32), lines)
    lines = lines.astype(BF16)
    _, oa = split_index((outn * rows, full), 0, rows)
    _, ob = split_index((outn * rows, full), 1, rows)
    wo[...] = jnp.where(oa == ob, dot_nt(lines, spread), 0.0).astype(BF16)
    shape = (2 * outn, 2 * chans)
    edge_side, edge_k = split_index(shape, 0, outn)
    edge_half, _ = split_index(shape, 1, chans)
    twice = jnp.concatenate([out_w[...].astype(F32)] * 2, axis=1)
    lines = jnp.zeros(shape, F32)
    for k in range(outn):
        lines = jnp.where(edge_k == k, twice[k : k + 1], lines)
    woe[...] = jnp.where(edge_side == edge_half, lines, 0.0).astype(BF16)
    skips.wait()
    parts = [slice(n, n + cols // 2) for n in range(0, cols, cols // 2)]

    def partner(d):
        if peers & (peers - 1):
            return lax.rem(me + d, peers)
        flipped, bit = 0, 1
        while bit < peers:
            flipped = flipped + bit * lax.rem(lax.div(me, bit) + (d // bit) % 2, 2)
            bit *= 2
        return flipped

    def edge_copy(d):
        return pltpu.make_async_remote_copy(
            src_ref=esend, dst_ref=yedge.at[d],
            send_sem=es_sem.at[d - 1], recv_sem=er_sem.at[d - 1],
            device_id={"member": partner(d)}, device_id_type=MESH,
        )

    others = range(peers - 1, 0, -1)
    edges = 2 * outn

    def gather_copy(m, part, d):
        return pltpu.make_async_remote_copy(
            src_ref=osend.at[m, :, parts[part]],
            dst_ref=ybuf.at[d, m, :, parts[part]],
            send_sem=as_sem.at[d - 1], recv_sem=ar_sem.at[d - 1],
            device_id={"member": partner(d)}, device_id_type=MESH,
        )

    def gather_whole(d):
        return pltpu.make_async_remote_copy(
            src_ref=osend, dst_ref=ybuf.at[d],
            send_sem=as_sem.at[d - 1], recv_sem=ar_sem.at[d - 1],
            device_id={"member": partner(d)}, device_id_type=MESH,
        )

    def project(m, part, values):
        for n, value in values:
            span = slice(n, n + chunk)
            value = dot(wo[...], value)
            outs[m, :, span] = value
            osend[m, :, span] = value.astype(BF16)
        for d in others:
            gather_copy(m, part, d).start()

    waiting = None
    for m in range(members):
        wide = widened(x, m, (-1, 0, 1))
        for part, range_of in enumerate(parts):
            values = []
            for n in range(range_of.start, range_of.stop, chunk):
                span = slice(n, n + chunk)
                total = convolve(wf, wide, span) + skip[m, :, span].astype(F32)
                put(m, span, total)
                pedge[m, :, span] = edge_rows(m, span)
                values.append((n, gelu_value(total).astype(BF16)))
            if waiting is not None:
                project(*waiting)
            waiting = (m, part, values)
    project(*waiting)

    halo_wait([(hs, hx, hs_sem, hx_sem)], "recv")
    for m in range(members):
        stack_halo(m, hx[0, m], hx[1, m], hstk, (-1, 0, 1))
    for m in range(members):
        for span in spans:
            total = pedge[m, :, span] + dot(wfh[...], hstk[m, :, span])
            put_edge_rows(m, span, total)
            value = dot(woe[...], gelu_value(total).astype(BF16))
            esend[m, :, span] = value.astype(BF16)
            oute[m * edges : (m + 1) * edges, span] = value
    for d in others:
        edge_copy(d).start()

    block = 8 * rows
    for m in range(members):
        for n in range(0, full, block):
            for span in spans:
                lines = slice(n, n + block)
                slope[m, lines, span] = gelu_slope(get(m, span, lines)).astype(BF16)
        extract_edges(m, slope[m], se)
    halo_start(se, hse, gs_sem, hg_sem)
    build_backward()
    build_edges(wbh, True)
    eye = (
        lax.broadcasted_iota(jnp.int32, (chans, chans), 0)
        == lax.broadcasted_iota(jnp.int32, (chans, chans), 1)
    ).astype(F32).astype(BF16)
    for k in range(outn):
        flat = jnp.broadcast_to(out_w[k : k + 1, :].astype(F32), (chunk, chans)).astype(BF16)
        wcol[k] = dot_nt(spread, flat).astype(BF16)
        wrow[k] = dot_nt(eye, flat[:lane])

    tgt.wait()
    total_members = peers * members
    for d in others:
        gather_whole(d).wait_recv()
    for part in range(2):
        for n in range(parts[part].start, parts[part].stop, chunk):
            span = slice(n, n + chunk)
            own = [outs[m, :, span] for m in range(members)]
            pairs = [smooth_slope(v - v) for v in own]
            for i in range(members):
                for j in range(i):
                    term = smooth_slope(own[i] - own[j])
                    pairs[i] = pairs[i] + term
                    pairs[j] = pairs[j] - term
            for d in range(1, peers):
                for j in range(members):
                    other = ybuf[d, j, :, span].astype(F32)
                    for i in range(members):
                        pairs[i] = pairs[i] + smooth_slope(own[i] - other)
            for i in range(members):
                grad = smooth_slope(own[i] - target[:, span]) - pairs[i] / (total_members - 1)
                for k in range(outn):
                    part_k = grad[k * rows : (k + 1) * rows]
                    gout[i, k, :, span] = part_k

    shape = (members * edges, edges)
    repeat = (
        split_index(shape, 0, edges)[1] == lax.broadcasted_iota(jnp.int32, shape, 1)
    ).astype(F32).astype(BF16)
    for m in range(members):
        for side in range(2):
            for k in range(outn):
                row = m * edges + side * outn + k
                from_row = k * rows + side * (rows - 1)
                tedge[row : row + 1, :] = target[from_row : from_row + 1, :]
    for d in others:
        edge_copy(d).wait_recv()
    for span in spans:
        own = oute[:, span]
        total = jnp.zeros(own.shape, F32)
        for j in range(members):
            other = jnp.concatenate([own[j * edges : (j + 1) * edges]] * members, axis=0)
            total = total + smooth_slope(own - other)
        for d in range(1, peers):
            for j in range(members):
                total = total + smooth_slope(own - dot(repeat, yedge[d, j, :, span]))
        grad = smooth_slope(own - tedge[:, span]) - total / (total_members - 1)
        for i in range(members):
            for side in range(2):
                row = i * edges + side * outn
                gsend[side, i, :, span] = grad[row : row + outn]
                for k in range(outn):
                    line = side * (rows - 1)
                    gout[i, k, line : line + 1, span] = grad[row + k : row + k + 1]

    halo_start(gsend, hgo, cs_sem, cr_sem)
    def activate(m, span):
        score = [gout[m, k, :, span].astype(BF16) for k in range(outn)]
        for n in range(0, full, rows):
            lines = slice(n, n + rows)
            grad = wcol[0, lines, :] * score[0]
            for k in range(1, outn):
                grad = grad + wcol[k, lines, :] * score[k]
            act[m, lines, span] = grad * slope[m, lines, span]

    for m in range(members):
        for span in spans:
            activate(m, span)
        wide = widened(act, m, (1, 0, -1))
        for span in spans:
            put(m, span, convolve(wb, wide, span))
    halo_wait([(hs, hx, hs_sem, hx_sem), (se, hse, gs_sem, hg_sem)], "send")
    for d in others:
        gather_whole(d).wait_send()
        edge_copy(d).wait_send()
    halo_wait([(se, hse, gs_sem, hg_sem), (gsend, hgo, cs_sem, cr_sem)], "recv")
    for m in range(members):
        both = []
        for half in range(2):
            tiles = []
            for c in range(0, cols, lane):
                span = slice(c, c + lane)
                grad = wrow[0] * hgo[half, m, 0:1, span].astype(BF16).astype(F32)
                for k in range(1, outn):
                    grad = grad + wrow[k] * hgo[half, m, k : k + 1, span].astype(BF16).astype(F32)
                tiles.append((grad * hse[half, m, :, span].astype(F32)).astype(BF16))
            both.append(jnp.concatenate(tiles, axis=1))
        stack_halo(m, both[0], both[1], hstk, (1, 0, -1))
        for span in spans:
            put_edge_rows(m, span, edge_rows(m, span) + dot(wbh[...], hstk[m, :, span]))

    halo_wait([(gsend, hgo, cs_sem, cr_sem)], "send")


def finish(dims, pre, out_hbm, out, sem):
    members, cols, chunk = dims
    copies = []
    for m in range(members):
        for n in range(0, cols, chunk):
            span = slice(n, n + chunk)
            tiles = [pre[m, (n + k) // lane] for k in range(0, chunk, lane)]
            out[m, :, span] = jnp.concatenate(tiles, axis=1).astype(BF16)
            copy = pltpu.make_async_copy(
                out.at[m, :, span], out_hbm.at[m, :, span], sem.at[m, n // chunk]
            )
            copy.start()
            copies.append(copy)
    for copy in copies:
        copy.wait()


def local(features, skip, conv_weight, out_weight, target):
    members, chans, rows, cols = features.shape
    outn = out_weight.shape[0]
    peers = lax.axis_size("member")
    count = lax.axis_size("space")
    full = chans * rows
    chunk = min(cols, 256)
    dims = (members, chans, rows, cols, peers, count, outn, chunk)
    dma = pltpu.SemaphoreType.DMA
    anywhere = pl.BlockSpec(memory_space=pltpu.HBM)
    vmem = pl.BlockSpec(memory_space=pltpu.VMEM)
    held = pl.pallas_call(
        functools.partial(kernel, dims),
        out_shape=pltpu.VMEM((members, cols // lane, full, lane), F32),
        in_specs=[anywhere] * 5,
        out_specs=vmem,
        scratch_shapes=[
            pltpu.VMEM((members, full, cols), BF16),
            pltpu.VMEM((members, full, cols), BF16),
            pltpu.VMEM(conv_weight.shape, BF16),
            pltpu.VMEM(out_weight.shape, BF16),
            pltpu.VMEM((outn * rows, cols), F32),
            pltpu.VMEM((members, 6 * chans, cols), BF16),
            pltpu.VMEM((members, full, cols), BF16),
            pltpu.VMEM((members, full, cols), BF16),
            pltpu.VMEM((2, members, chans, cols), BF16),
            pltpu.VMEM((2, members, chans, cols), BF16),
            pltpu.VMEM((2, members, chans, cols), BF16),
            pltpu.VMEM((2, members, outn, cols), F32),
            pltpu.VMEM((members, outn * rows, cols), F32),
            pltpu.VMEM((members, outn * rows, cols), BF16),
            pltpu.VMEM((peers, members, outn * rows, cols), BF16),
            pltpu.VMEM((members, 2 * outn, cols), BF16),
            pltpu.VMEM((peers, members, 2 * outn, cols), BF16),
            pltpu.VMEM((members * 2 * outn, cols), F32),
            pltpu.VMEM((members * 2 * outn, cols), F32),
            pltpu.VMEM((members, 2 * chans, cols), F32),
            pltpu.VMEM((members, outn, rows, cols), F32),
            pltpu.VMEM((2, members, outn, cols), F32),
            pltpu.VMEM((2, members, chans, cols), BF16),
            pltpu.VMEM((full, 3 * full), BF16),
            pltpu.VMEM((2 * chans, 6 * chans), BF16),
            pltpu.VMEM((full, 3 * full), BF16),
            pltpu.VMEM((2 * chans, 6 * chans), BF16),
            pltpu.VMEM((3, full // lane, full, lane), F32),
            pltpu.VMEM((outn * rows, full), BF16),
            pltpu.VMEM((2 * outn, 2 * chans), BF16),
            pltpu.VMEM((outn, full, chunk), BF16),
            pltpu.VMEM((outn, chans, lane), F32),
            pltpu.VMEM((2 * chans, full), BF16),
            dma((members + 4,)),
            dma((2,)),
            dma((2,)),
            dma((2,)),
            dma((2,)),
            dma((peers - 1,)),
            dma((peers - 1,)),
            dma((peers - 1,)),
            dma((peers - 1,)),
            dma((2,)),
            dma((2,)),
        ],
        compiler_params=pltpu.CompilerParams(collective_id=0, has_side_effects=True, vmem_limit_bytes=58 * 2**20),
    )(
        features.reshape(members, full, cols),
        skip.reshape(members, full, cols),
        conv_weight,
        out_weight,
        target.reshape(outn * rows, cols),
    )
    result = pl.pallas_call(
        functools.partial(finish, (members, cols, chunk)),
        out_shape=jax.ShapeDtypeStruct((members, full, cols), BF16),
        in_specs=[vmem],
        out_specs=anywhere,
        scratch_shapes=[pltpu.VMEM((members, full, cols), BF16), dma((members, cols // chunk))],
        compiler_params=pltpu.CompilerParams(vmem_limit_bytes=16 * 2**20),
    )(held)
    return result.reshape(members, chans, rows, cols)


def solution(mesh):
    placed = (
        P("member", None, "space", None),
        P("member", None, "space", None),
        P(),
        P(),
        P(None, "space", None),
    )
    return jax.shard_map(
        local,
        mesh=mesh,
        in_specs=placed,
        out_specs=P("member", None, "space", None),
        check_vma=False,
    )
```

```python
import functools
import math

import jax
import jax.numpy as jnp
from jax import lax
from jax.experimental import pallas as pl
from jax.experimental.pallas import tpu as pltpu
from jax.sharding import PartitionSpec as P

root_coef = math.sqrt(2.0 / math.pi)
cubic_coef = 0.044715
smooth = 0.25
lane = 128
MESH = pl.DeviceIdType.MESH
F32 = jnp.float32
BF16 = jnp.bfloat16


def gelu_half(source, square):
    return 0.5 + 0.5 * jnp.tanh(source * (root_coef + (root_coef * cubic_coef) * square))


def gelu_value(source):
    return source * gelu_half(source, source * source)


def gelu_slope(source):
    square = source * source
    half = gelu_half(source, square)
    rate = 2.0 * root_coef + (6.0 * root_coef * cubic_coef) * square
    return half + (source * half) * ((1.0 - half) * rate)


def smooth_slope(source):
    return source * lax.rsqrt(source * source + smooth * smooth)


def dot(left, right):
    return lax.dot_general(left, right, (((1,), (0,)), ((), ())), preferred_element_type=F32)


def dot_nt(left, right):
    return lax.dot_general(left, right, (((1,), (1,)), ((), ())), preferred_element_type=F32)


def split_index(shape, dim, size):
    index = lax.broadcasted_iota(jnp.int32, shape, dim)
    if size & (size - 1) == 0:
        return lax.shift_right_logical(index, size.bit_length() - 1), index & (size - 1)
    return lax.div(index, size), lax.rem(index, size)


def shifted(value, step):
    count = value.shape[1]
    edge = jnp.zeros((value.shape[0], 1), value.dtype)
    if step == 1:
        return jnp.concatenate([value[:, 1:], edge], axis=1)
    return jnp.concatenate([edge, value[:, : count - 1]], axis=1)


def kernel(
    dims, x_hbm, skip_hbm, weight_hbm, out_w_hbm, target_hbm, pre,
    x, skip, weight, out_w, target, act, slope, hs, hx, hse, hgo, outs, osend, ybuf, esend, yedge, oute, tedge, pedge,
    gout, gsend, se, wf, wfh, wb, wbh, band, wo, woe, wcol, wrow, sel,
    in_sem, hs_sem, hx_sem, gs_sem, hg_sem, as_sem, ar_sem, es_sem, er_sem, cs_sem, cr_sem,
):
    members, chans, rows, cols, peers, count, outn, chunk = dims
    full = chans * rows
    me = lax.axis_index("member")
    at = lax.axis_index("space")
    has_up = at > 0
    has_dn = at < count - 1
    up = {"space": lax.max(at - 1, 0)}
    dn = {"space": lax.min(at + 1, count - 1)}

    loads = [pltpu.make_async_copy(x_hbm.at[m], x.at[m], in_sem.at[m]) for m in range(members)]
    skips = pltpu.make_async_copy(skip_hbm, skip, in_sem.at[members])
    tgt = pltpu.make_async_copy(target_hbm, target, in_sem.at[members + 1])
    taps = pltpu.make_async_copy(weight_hbm, weight, in_sem.at[members + 2])
    heads = pltpu.make_async_copy(out_w_hbm, out_w, in_sem.at[members + 3])
    for c in loads[:1] + [taps, heads] + loads[1:] + [skips, tgt]:
        c.start()

    barrier = pltpu.get_barrier_semaphore()
    for d in range(1, peers):
        pl.semaphore_signal(
            barrier, inc=1, device_id={"member": lax.rem(me + d, peers)}, device_id_type=MESH
        )

    @pl.when(has_up)
    def _():
        pl.semaphore_signal(barrier, inc=1, device_id=up, device_id_type=MESH)

    @pl.when(has_dn)
    def _():
        pl.semaphore_signal(barrier, inc=1, device_id=dn, device_id_type=MESH)

    chan, row = split_index((2 * chans, full), 1, rows)
    half, pick = split_index((2 * chans, full), 0, chans)
    sel[...] = (
        (chan == pick) & (row == jnp.where(half == 0, 0, rows - 1))
    ).astype(F32).astype(BF16)

    left_chan, _ = split_index((full, chans), 0, rows)
    spread = (left_chan == lax.broadcasted_iota(jnp.int32, (full, chans), 1)).astype(F32)
    spread = spread.astype(BF16)

    def build_forward():
        taps.wait()
        wide = dot_nt(weight[...].reshape(9 * chans, chans), spread)
        lane_row = lax.broadcasted_iota(jnp.int32, (chans, lane), 1) & (rows - 1)
        for dc in range(3):
            for tile in range(full // lane):
                cut = slice(tile * lane, (tile + 1) * lane)
                tap = [wide[(3 * dr + dc) * chans : (3 * dr + dc + 1) * chans, cut] for dr in range(3)]
                for r in range(rows):
                    line = jnp.where(lane_row == r, tap[1], 0.0)
                    if r > 0:
                        line = jnp.where(lane_row == r - 1, tap[0], line)
                    if r < rows - 1:
                        line = jnp.where(lane_row == r + 1, tap[2], line)
                    band[dc, tile, pl.ds(r, chans, stride=rows), :] = line
                wf[:, dc * full + tile * lane : dc * full + (tile + 1) * lane] = band[
                    dc, tile
                ].astype(BF16)

    def build_edges(halo, flipped):
        pieces = []
        for dc in range(3):
            for dr in (2, 0) if flipped else (0, 2):
                tap = weight[dr, dc].astype(F32)
                pieces.append(tap.T if flipped else tap)
        line = jnp.concatenate(pieces, axis=1)
        slot, _ = split_index((chans, 6 * chans), 1, chans)
        first = jnp.where(slot & 1 == 0, line, 0.0).astype(BF16)
        last = jnp.where(slot & 1 == 1, line, 0.0).astype(BF16)
        halo[...] = jnp.concatenate([first, last], axis=0)

    def build_backward():
        for dc in range(3):
            span = slice(dc * full, (dc + 1) * full)
            wb[:, span] = wf[:, span].T

    for absent, side in ((jnp.logical_not(has_up), 0), (jnp.logical_not(has_dn), 1)):

        @pl.when(absent)
        def _(side=side):
            for landing in (hx, hse, hgo):
                for m in range(members):
                    landing[side, m] = jnp.zeros(landing.shape[2:], landing.dtype)

    def halo_copies(src, dst, send, recv):
        to_up = pltpu.make_async_remote_copy(
            src_ref=src.at[0], dst_ref=dst.at[1], send_sem=send.at[0],
            recv_sem=recv.at[1], device_id=up, device_id_type=MESH,
        )
        to_dn = pltpu.make_async_remote_copy(
            src_ref=src.at[1], dst_ref=dst.at[0], send_sem=send.at[1],
            recv_sem=recv.at[0], device_id=dn, device_id_type=MESH,
        )
        return to_up, to_dn

    def halo_start(*exchange):
        to_up, to_dn = halo_copies(*exchange)

        @pl.when(has_up)
        def _():
            to_up.start()

        @pl.when(has_dn)
        def _():
            to_dn.start()

    def halo_wait(exchanges, kind):
        copies = [halo_copies(*exchange) for exchange in exchanges]

        @pl.when(has_up)
        def _():
            for to_up, to_dn in copies:
                to_up.wait_send() if kind == "send" else to_dn.wait_recv()

        @pl.when(has_dn)
        def _():
            for to_up, to_dn in copies:
                to_dn.wait_send() if kind == "send" else to_up.wait_recv()

    def extract_edges(m, source, store):
        edge = dot(sel[...], source).astype(BF16)
        store[0, m] = edge[:chans]
        store[1, m] = edge[chans:]

    def stacked(above, below, order):
        both = jnp.concatenate([above, below], axis=0)
        return jnp.concatenate(
            [both if step == 0 else shifted(both, step) for step in order], axis=0
        )

    def widened(src, m, order):
        value = src[m]
        return [value if step == 0 else shifted(value, step) for step in order]

    def convolve(taps, wide, span):
        return dot(taps[...], jnp.concatenate([value[:, span] for value in wide], axis=0))

    def edge_rows(m, span):
        tiles = range(span.start // lane, span.stop // lane)
        halves = [
            jnp.concatenate(
                [pre[m, t, pl.ds(side * (rows - 1), chans, stride=rows), :] for t in tiles], axis=1
            )
            for side in range(2)
        ]
        return jnp.concatenate(halves, axis=0)

    def put_edge_rows(m, span, value):
        for side in range(2):
            for k, t in enumerate(range(span.start // lane, span.stop // lane)):
                pre[m, t, pl.ds(side * (rows - 1), chans, stride=rows), :] = value[
                    side * chans : (side + 1) * chans, k * lane : (k + 1) * lane
                ]

    spans = [slice(n, n + chunk) for n in range(0, cols, chunk)]

    def get(m, span, lines=slice(None)):
        tiles = range(span.start // lane, span.stop // lane)
        return jnp.concatenate([pre[m, tile, lines, :] for tile in tiles], axis=1)

    def put(m, span, value, lines=slice(None)):
        for k, tile in enumerate(range(span.start // lane, span.stop // lane)):
            pre[m, tile, lines, :] = value[:, k * lane : (k + 1) * lane]

    for m in range(members):
        loads[m].wait()
        extract_edges(m, x[m], hs)
    pl.semaphore_wait(
        barrier, peers - 1 + has_up.astype(jnp.int32) + has_dn.astype(jnp.int32)
    )
    halo_start(hs, hx, hs_sem, hx_sem)
    build_forward()
    build_edges(wfh, False)
    heads.wait()

    out_k, _ = split_index((outn * rows, chans), 0, rows)
    lines = jnp.zeros((outn * rows, chans), F32)
    for k in range(outn):
        lines = jnp.where(out_k == k, out_w[k : k + 1, :].astype(F32), lines)
    lines = lines.astype(BF16)
    _, oa = split_index((outn * rows, full), 0, rows)
    _, ob = split_index((outn * rows, full), 1, rows)
    wo[...] = jnp.where(oa == ob, dot_nt(lines, spread), 0.0).astype(BF16)
    shape = (2 * outn, 2 * chans)
    edge_side, edge_k = split_index(shape, 0, outn)
    edge_half, _ = split_index(shape, 1, chans)
    twice = jnp.concatenate([out_w[...].astype(F32)] * 2, axis=1)
    lines = jnp.zeros(shape, F32)
    for k in range(outn):
        lines = jnp.where(edge_k == k, twice[k : k + 1], lines)
    woe[...] = jnp.where(edge_side == edge_half, lines, 0.0).astype(BF16)
    skips.wait()
    parts = [slice(n, n + cols // 2) for n in range(0, cols, cols // 2)]

    def partner(d):
        if peers & (peers - 1):
            return lax.rem(me + d, peers)
        flipped, bit = 0, 1
        while bit < peers:
            flipped = flipped + bit * lax.rem(lax.div(me, bit) + (d // bit) % 2, 2)
            bit *= 2
        return flipped

    def edge_copy(d):
        return pltpu.make_async_remote_copy(
            src_ref=esend, dst_ref=yedge.at[d],
            send_sem=es_sem.at[d - 1], recv_sem=er_sem.at[d - 1],
            device_id={"member": partner(d)}, device_id_type=MESH,
        )

    others = range(peers - 1, 0, -1)
    edges = 2 * outn

    def gather_copy(m, part, d):
        return pltpu.make_async_remote_copy(
            src_ref=osend.at[m, :, parts[part]],
            dst_ref=ybuf.at[d, m, :, parts[part]],
            send_sem=as_sem.at[d - 1], recv_sem=ar_sem.at[d - 1],
            device_id={"member": partner(d)}, device_id_type=MESH,
        )

    def gather_whole(d):
        return pltpu.make_async_remote_copy(
            src_ref=osend, dst_ref=ybuf.at[d],
            send_sem=as_sem.at[d - 1], recv_sem=ar_sem.at[d - 1],
            device_id={"member": partner(d)}, device_id_type=MESH,
        )

    def project(m, part, values):
        for n, value in values:
            span = slice(n, n + chunk)
            value = dot(wo[...], value)
            outs[m, :, span] = value
            osend[m, :, span] = value.astype(BF16)
        for d in others:
            gather_copy(m, part, d).start()

    waiting = None
    for m in range(members):
        wide = widened(x, m, (-1, 0, 1))
        for part, range_of in enumerate(parts):
            values = []
            for n in range(range_of.start, range_of.stop, chunk):
                span = slice(n, n + chunk)
                total = convolve(wf, wide, span) + skip[m, :, span].astype(F32)
                put(m, span, total)
                pedge[m, :, span] = edge_rows(m, span)
                values.append((n, gelu_value(total).astype(BF16)))
            if waiting is not None:
                project(*waiting)
            waiting = (m, part, values)
    project(*waiting)

    halo_wait([(hs, hx, hs_sem, hx_sem)], "recv")
    halos = [stacked(hx[0, m], hx[1, m], (-1, 0, 1)) for m in range(members)]
    work = [(m, span) for m in range(members) for span in spans]
    totals, values = {}, {}
    for step in range(len(work) + 2):
        if step < len(work):
            m, span = work[step]
            totals[step] = pedge[m, :, span] + dot(wfh[...], halos[m][:, span])
        if 1 <= step <= len(work):
            m, span = work[step - 1]
            total = totals.pop(step - 1)
            put_edge_rows(m, span, total)
            values[step - 1] = gelu_value(total).astype(BF16)
        if step >= 2:
            m, span = work[step - 2]
            value = dot(woe[...], values.pop(step - 2))
            esend[m, :, span] = value.astype(BF16)
            oute[m * edges : (m + 1) * edges, span] = value
    for d in others:
        edge_copy(d).start()

    block = 8 * rows
    for m in range(members):
        for n in range(0, full, block):
            for span in spans:
                lines = slice(n, n + block)
                slope[m, lines, span] = gelu_slope(get(m, span, lines)).astype(BF16)
        extract_edges(m, slope[m], se)
    halo_start(se, hse, gs_sem, hg_sem)
    build_backward()
    build_edges(wbh, True)
    eye = (
        lax.broadcasted_iota(jnp.int32, (chans, chans), 0)
        == lax.broadcasted_iota(jnp.int32, (chans, chans), 1)
    ).astype(F32).astype(BF16)
    for k in range(outn):
        flat = jnp.broadcast_to(out_w[k : k + 1, :].astype(F32), (chunk, chans)).astype(BF16)
        wcol[k] = dot_nt(spread, flat).astype(BF16)
        wrow[k] = dot_nt(eye, flat[:lane])

    tgt.wait()
    total_members = peers * members
    for d in others:
        gather_whole(d).wait_recv()
    for part in range(2):
        for n in range(parts[part].start, parts[part].stop, chunk):
            span = slice(n, n + chunk)
            own = [outs[m, :, span] for m in range(members)]
            pairs = [smooth_slope(v - v) for v in own]
            for i in range(members):
                for j in range(i):
                    term = smooth_slope(own[i] - own[j])
                    pairs[i] = pairs[i] + term
                    pairs[j] = pairs[j] - term
            for d in range(1, peers):
                for j in range(members):
                    other = ybuf[d, j, :, span].astype(F32)
                    for i in range(members):
                        pairs[i] = pairs[i] + smooth_slope(own[i] - other)
            for i in range(members):
                grad = smooth_slope(own[i] - target[:, span]) - pairs[i] / (total_members - 1)
                for k in range(outn):
                    part_k = grad[k * rows : (k + 1) * rows]
                    gout[i, k, :, span] = part_k

    shape = (members * edges, edges)
    repeat = (
        split_index(shape, 0, edges)[1] == lax.broadcasted_iota(jnp.int32, shape, 1)
    ).astype(F32).astype(BF16)
    for m in range(members):
        for side in range(2):
            for k in range(outn):
                row = m * edges + side * outn + k
                from_row = k * rows + side * (rows - 1)
                tedge[row : row + 1, :] = target[from_row : from_row + 1, :]
    for d in others:
        edge_copy(d).wait_recv()
    for span in spans:
        own = oute[:, span]
        total = jnp.zeros(own.shape, F32)
        for j in range(members):
            other = jnp.concatenate([own[j * edges : (j + 1) * edges]] * members, axis=0)
            total = total + smooth_slope(own - other)
        for d in range(1, peers):
            for j in range(members):
                total = total + smooth_slope(own - dot(repeat, yedge[d, j, :, span]))
        grad = smooth_slope(own - tedge[:, span]) - total / (total_members - 1)
        for i in range(members):
            for side in range(2):
                row = i * edges + side * outn
                gsend[side, i, :, span] = grad[row : row + outn]
                for k in range(outn):
                    line = side * (rows - 1)
                    gout[i, k, line : line + 1, span] = grad[row + k : row + k + 1]

    halo_start(gsend, hgo, cs_sem, cr_sem)
    def activate(m, span):
        score = [gout[m, k, :, span].astype(BF16) for k in range(outn)]
        for n in range(0, full, rows):
            lines = slice(n, n + rows)
            grad = wcol[0, lines, :] * score[0]
            for k in range(1, outn):
                grad = grad + wcol[k, lines, :] * score[k]
            act[m, lines, span] = grad * slope[m, lines, span]

    for m in range(members):
        for span in spans:
            activate(m, span)
        wide = widened(act, m, (1, 0, -1))
        for span in spans:
            put(m, span, convolve(wb, wide, span))
    halo_wait([(hs, hx, hs_sem, hx_sem), (se, hse, gs_sem, hg_sem)], "send")
    for d in others:
        gather_whole(d).wait_send()
        edge_copy(d).wait_send()
    halo_wait([(se, hse, gs_sem, hg_sem), (gsend, hgo, cs_sem, cr_sem)], "recv")
    halos = []
    for m in range(members):
        both = []
        for half in range(2):
            tiles = []
            for c in range(0, cols, lane):
                span = slice(c, c + lane)
                grad = wrow[0] * hgo[half, m, 0:1, span].astype(BF16).astype(F32)
                for k in range(1, outn):
                    grad = grad + wrow[k] * hgo[half, m, k : k + 1, span].astype(BF16).astype(F32)
                tiles.append((grad * hse[half, m, :, span].astype(F32)).astype(BF16))
            both.append(jnp.concatenate(tiles, axis=1))
        halos.append(stacked(both[0], both[1], (1, 0, -1)))
    for step in range(len(work) + 1):
        if step < len(work):
            m, span = work[step]
            totals[step] = edge_rows(m, span) + dot(wbh[...], halos[m][:, span])
        if step >= 1:
            m, span = work[step - 1]
            put_edge_rows(m, span, totals.pop(step - 1))

    halo_wait([(gsend, hgo, cs_sem, cr_sem)], "send")


def finish(dims, pre, out_hbm, out, sem):
    members, cols, chunk = dims
    copies = []
    for m in range(members):
        for n in range(0, cols, chunk):
            span = slice(n, n + chunk)
            tiles = [pre[m, (n + k) // lane] for k in range(0, chunk, lane)]
            out[m, :, span] = jnp.concatenate(tiles, axis=1).astype(BF16)
            copy = pltpu.make_async_copy(
                out.at[m, :, span], out_hbm.at[m, :, span], sem.at[m, n // chunk]
            )
            copy.start()
            copies.append(copy)
    for copy in copies:
        copy.wait()


def local(features, skip, conv_weight, out_weight, target):
    members, chans, rows, cols = features.shape
    outn = out_weight.shape[0]
    peers = lax.axis_size("member")
    count = lax.axis_size("space")
    full = chans * rows
    chunk = min(cols, 256)
    dims = (members, chans, rows, cols, peers, count, outn, chunk)
    dma = pltpu.SemaphoreType.DMA
    anywhere = pl.BlockSpec(memory_space=pltpu.HBM)
    vmem = pl.BlockSpec(memory_space=pltpu.VMEM)
    held = pl.pallas_call(
        functools.partial(kernel, dims),
        out_shape=pltpu.VMEM((members, cols // lane, full, lane), F32),
        in_specs=[anywhere] * 5,
        out_specs=vmem,
        scratch_shapes=[
            pltpu.VMEM((members, full, cols), BF16),
            pltpu.VMEM((members, full, cols), BF16),
            pltpu.VMEM(conv_weight.shape, BF16),
            pltpu.VMEM(out_weight.shape, BF16),
            pltpu.VMEM((outn * rows, cols), F32),
            pltpu.VMEM((members, full, cols), BF16),
            pltpu.VMEM((members, full, cols), BF16),
            pltpu.VMEM((2, members, chans, cols), BF16),
            pltpu.VMEM((2, members, chans, cols), BF16),
            pltpu.VMEM((2, members, chans, cols), BF16),
            pltpu.VMEM((2, members, outn, cols), F32),
            pltpu.VMEM((members, outn * rows, cols), F32),
            pltpu.VMEM((members, outn * rows, cols), BF16),
            pltpu.VMEM((peers, members, outn * rows, cols), BF16),
            pltpu.VMEM((members, 2 * outn, cols), BF16),
            pltpu.VMEM((peers, members, 2 * outn, cols), BF16),
            pltpu.VMEM((members * 2 * outn, cols), F32),
            pltpu.VMEM((members * 2 * outn, cols), F32),
            pltpu.VMEM((members, 2 * chans, cols), F32),
            pltpu.VMEM((members, outn, rows, cols), F32),
            pltpu.VMEM((2, members, outn, cols), F32),
            pltpu.VMEM((2, members, chans, cols), BF16),
            pltpu.VMEM((full, 3 * full), BF16),
            pltpu.VMEM((2 * chans, 6 * chans), BF16),
            pltpu.VMEM((full, 3 * full), BF16),
            pltpu.VMEM((2 * chans, 6 * chans), BF16),
            pltpu.VMEM((3, full // lane, full, lane), F32),
            pltpu.VMEM((outn * rows, full), BF16),
            pltpu.VMEM((2 * outn, 2 * chans), BF16),
            pltpu.VMEM((outn, full, chunk), BF16),
            pltpu.VMEM((outn, chans, lane), F32),
            pltpu.VMEM((2 * chans, full), BF16),
            dma((members + 4,)),
            dma((2,)),
            dma((2,)),
            dma((2,)),
            dma((2,)),
            dma((peers - 1,)),
            dma((peers - 1,)),
            dma((peers - 1,)),
            dma((peers - 1,)),
            dma((2,)),
            dma((2,)),
        ],
        compiler_params=pltpu.CompilerParams(collective_id=0, has_side_effects=True, vmem_limit_bytes=58 * 2**20),
    )(
        features.reshape(members, full, cols),
        skip.reshape(members, full, cols),
        conv_weight,
        out_weight,
        target.reshape(outn * rows, cols),
    )
    result = pl.pallas_call(
        functools.partial(finish, (members, cols, chunk)),
        out_shape=jax.ShapeDtypeStruct((members, full, cols), BF16),
        in_specs=[vmem],
        out_specs=anywhere,
        scratch_shapes=[pltpu.VMEM((members, full, cols), BF16), dma((members, cols // chunk))],
        compiler_params=pltpu.CompilerParams(vmem_limit_bytes=16 * 2**20),
    )(held)
    return result.reshape(members, chans, rows, cols)


def solution(mesh):
    placed = (
        P("member", None, "space", None),
        P("member", None, "space", None),
        P(),
        P(),
        P(None, "space", None),
    )
    return jax.shard_map(
        local,
        mesh=mesh,
        in_specs=placed,
        out_specs=P("member", None, "space", None),
        check_vma=False,
    )
```

```python
import functools
import math

import jax
import jax.numpy as jnp
from jax import lax
from jax.experimental import pallas as pl
from jax.experimental.pallas import tpu as pltpu
from jax.sharding import PartitionSpec as P

root_coef = math.sqrt(2.0 / math.pi)
cubic_coef = 0.044715
smooth = 0.25
lane = 128
MESH = pl.DeviceIdType.MESH
F32 = jnp.float32
BF16 = jnp.bfloat16


def gelu_half(source, square):
    return 0.5 + 0.5 * jnp.tanh(source * (root_coef + (root_coef * cubic_coef) * square))


def gelu_value(source):
    return source * gelu_half(source, source * source)


def gelu_slope(source):
    square = source * source
    half = gelu_half(source, square)
    rate = 2.0 * root_coef + (6.0 * root_coef * cubic_coef) * square
    return half + (source * half) * ((1.0 - half) * rate)


def smooth_slope(source):
    return source * lax.rsqrt(source * source + smooth * smooth)


def dot(left, right):
    return lax.dot_general(left, right, (((1,), (0,)), ((), ())), preferred_element_type=F32)


def dot_nt(left, right):
    return lax.dot_general(left, right, (((1,), (1,)), ((), ())), preferred_element_type=F32)


def split_index(shape, dim, size):
    index = lax.broadcasted_iota(jnp.int32, shape, dim)
    if size & (size - 1) == 0:
        return lax.shift_right_logical(index, size.bit_length() - 1), index & (size - 1)
    return lax.div(index, size), lax.rem(index, size)


def shifted(value, step):
    count = value.shape[1]
    edge = jnp.zeros((value.shape[0], 1), value.dtype)
    if step == 1:
        return jnp.concatenate([value[:, 1:], edge], axis=1)
    return jnp.concatenate([edge, value[:, : count - 1]], axis=1)


def kernel(
    dims, x_hbm, skip_hbm, weight_hbm, out_w_hbm, target_hbm, pre,
    x, skip, weight, out_w, target, act, slope, hs, hx, hse, hgo, outs, osend, ybuf, esend, yedge, oute, tedge, pedge,
    gout, gsend, se, wf, wfh, wb, wbh, band, wo, woe, wcol, wrow, sel,
    in_sem, hs_sem, hx_sem, gs_sem, hg_sem, as_sem, ar_sem, es_sem, er_sem, cs_sem, cr_sem,
):
    members, chans, rows, cols, peers, count, outn, chunk = dims
    full = chans * rows
    me = lax.axis_index("member")
    at = lax.axis_index("space")
    has_up = at > 0
    has_dn = at < count - 1
    up = {"space": lax.max(at - 1, 0)}
    dn = {"space": lax.min(at + 1, count - 1)}

    loads = [pltpu.make_async_copy(x_hbm.at[m], x.at[m], in_sem.at[m]) for m in range(members)]
    skips = pltpu.make_async_copy(skip_hbm, skip, in_sem.at[members])
    tgt = pltpu.make_async_copy(target_hbm, target, in_sem.at[members + 1])
    taps = pltpu.make_async_copy(weight_hbm, weight, in_sem.at[members + 2])
    heads = pltpu.make_async_copy(out_w_hbm, out_w, in_sem.at[members + 3])
    for c in loads[:1] + [taps, heads] + loads[1:] + [skips, tgt]:
        c.start()

    barrier = pltpu.get_barrier_semaphore()
    for d in range(1, peers):
        pl.semaphore_signal(
            barrier, inc=1, device_id={"member": lax.rem(me + d, peers)}, device_id_type=MESH
        )

    @pl.when(has_up)
    def _():
        pl.semaphore_signal(barrier, inc=1, device_id=up, device_id_type=MESH)

    @pl.when(has_dn)
    def _():
        pl.semaphore_signal(barrier, inc=1, device_id=dn, device_id_type=MESH)

    chan, row = split_index((2 * chans, full), 1, rows)
    half, pick = split_index((2 * chans, full), 0, chans)
    sel[...] = (
        (chan == pick) & (row == jnp.where(half == 0, 0, rows - 1))
    ).astype(F32).astype(BF16)

    left_chan, _ = split_index((full, chans), 0, rows)
    spread = (left_chan == lax.broadcasted_iota(jnp.int32, (full, chans), 1)).astype(F32)
    spread = spread.astype(BF16)

    def build_forward():
        taps.wait()
        wide = dot_nt(weight[...].reshape(9 * chans, chans), spread)
        lane_row = lax.broadcasted_iota(jnp.int32, (chans, lane), 1) & (rows - 1)
        for dc in range(3):
            for tile in range(full // lane):
                cut = slice(tile * lane, (tile + 1) * lane)
                tap = [wide[(3 * dr + dc) * chans : (3 * dr + dc + 1) * chans, cut] for dr in range(3)]
                for r in range(rows):
                    line = jnp.where(lane_row == r, tap[1], 0.0)
                    if r > 0:
                        line = jnp.where(lane_row == r - 1, tap[0], line)
                    if r < rows - 1:
                        line = jnp.where(lane_row == r + 1, tap[2], line)
                    band[dc, tile, pl.ds(r, chans, stride=rows), :] = line
                wf[:, dc * full + tile * lane : dc * full + (tile + 1) * lane] = band[
                    dc, tile
                ].astype(BF16)

    def build_edges(halo, flipped):
        pieces = []
        for dc in range(3):
            for dr in (2, 0) if flipped else (0, 2):
                tap = weight[dr, dc].astype(F32)
                pieces.append(tap.T if flipped else tap)
        line = jnp.concatenate(pieces, axis=1)
        slot, _ = split_index((chans, 6 * chans), 1, chans)
        first = jnp.where(slot & 1 == 0, line, 0.0).astype(BF16)
        last = jnp.where(slot & 1 == 1, line, 0.0).astype(BF16)
        halo[...] = jnp.concatenate([first, last], axis=0)

    def build_backward():
        for dc in range(3):
            span = slice(dc * full, (dc + 1) * full)
            wb[:, span] = wf[:, span].T

    for absent, side in ((jnp.logical_not(has_up), 0), (jnp.logical_not(has_dn), 1)):

        @pl.when(absent)
        def _(side=side):
            for landing in (hx, hse, hgo):
                for m in range(members):
                    landing[side, m] = jnp.zeros(landing.shape[2:], landing.dtype)

    def halo_copies(src, dst, send, recv):
        to_up = pltpu.make_async_remote_copy(
            src_ref=src.at[0], dst_ref=dst.at[1], send_sem=send.at[0],
            recv_sem=recv.at[1], device_id=up, device_id_type=MESH,
        )
        to_dn = pltpu.make_async_remote_copy(
            src_ref=src.at[1], dst_ref=dst.at[0], send_sem=send.at[1],
            recv_sem=recv.at[0], device_id=dn, device_id_type=MESH,
        )
        return to_up, to_dn

    def halo_start(*exchange):
        to_up, to_dn = halo_copies(*exchange)

        @pl.when(has_up)
        def _():
            to_up.start()

        @pl.when(has_dn)
        def _():
            to_dn.start()

    def halo_wait(exchanges, kind):
        copies = [halo_copies(*exchange) for exchange in exchanges]

        @pl.when(has_up)
        def _():
            for to_up, to_dn in copies:
                to_up.wait_send() if kind == "send" else to_dn.wait_recv()

        @pl.when(has_dn)
        def _():
            for to_up, to_dn in copies:
                to_dn.wait_send() if kind == "send" else to_up.wait_recv()

    def extract_edges(m, source, store):
        edge = dot(sel[...], source).astype(BF16)
        store[0, m] = edge[:chans]
        store[1, m] = edge[chans:]

    def stacked(above, below, order):
        both = jnp.concatenate([above, below], axis=0)
        return jnp.concatenate(
            [both if step == 0 else shifted(both, step) for step in order], axis=0
        )

    def widened(src, m, order):
        value = src[m]
        return [value if step == 0 else shifted(value, step) for step in order]

    def convolve(taps, wide, span):
        return dot(taps[...], jnp.concatenate([value[:, span] for value in wide], axis=0))

    def edge_rows(m, span):
        tiles = range(span.start // lane, span.stop // lane)
        halves = [
            jnp.concatenate(
                [pre[m, t, pl.ds(side * (rows - 1), chans, stride=rows), :] for t in tiles], axis=1
            )
            for side in range(2)
        ]
        return jnp.concatenate(halves, axis=0)

    def put_edge_rows(m, span, value):
        for side in range(2):
            for k, t in enumerate(range(span.start // lane, span.stop // lane)):
                pre[m, t, pl.ds(side * (rows - 1), chans, stride=rows), :] = value[
                    side * chans : (side + 1) * chans, k * lane : (k + 1) * lane
                ]

    spans = [slice(n, n + chunk) for n in range(0, cols, chunk)]

    def get(m, span, lines=slice(None)):
        tiles = range(span.start // lane, span.stop // lane)
        return jnp.concatenate([pre[m, tile, lines, :] for tile in tiles], axis=1)

    def put(m, span, value, lines=slice(None)):
        for k, tile in enumerate(range(span.start // lane, span.stop // lane)):
            pre[m, tile, lines, :] = value[:, k * lane : (k + 1) * lane]

    for m in range(members):
        loads[m].wait()
        extract_edges(m, x[m], hs)
    pl.semaphore_wait(
        barrier, peers - 1 + has_up.astype(jnp.int32) + has_dn.astype(jnp.int32)
    )
    halo_start(hs, hx, hs_sem, hx_sem)
    build_forward()
    build_edges(wfh, False)
    heads.wait()

    out_k, _ = split_index((outn * rows, chans), 0, rows)
    lines = jnp.zeros((outn * rows, chans), F32)
    for k in range(outn):
        lines = jnp.where(out_k == k, out_w[k : k + 1, :].astype(F32), lines)
    lines = lines.astype(BF16)
    _, oa = split_index((outn * rows, full), 0, rows)
    _, ob = split_index((outn * rows, full), 1, rows)
    wo[...] = jnp.where(oa == ob, dot_nt(lines, spread), 0.0).astype(BF16)
    shape = (2 * outn, 2 * chans)
    edge_side, edge_k = split_index(shape, 0, outn)
    edge_half, _ = split_index(shape, 1, chans)
    twice = jnp.concatenate([out_w[...].astype(F32)] * 2, axis=1)
    lines = jnp.zeros(shape, F32)
    for k in range(outn):
        lines = jnp.where(edge_k == k, twice[k : k + 1], lines)
    woe[...] = jnp.where(edge_side == edge_half, lines, 0.0).astype(BF16)
    skips.wait()
    parts = [slice(n, n + cols // 2) for n in range(0, cols, cols // 2)]

    def partner(d):
        if peers & (peers - 1):
            return lax.rem(me + d, peers)
        flipped, bit = 0, 1
        while bit < peers:
            flipped = flipped + bit * lax.rem(lax.div(me, bit) + (d // bit) % 2, 2)
            bit *= 2
        return flipped

    def edge_copy(d):
        return pltpu.make_async_remote_copy(
            src_ref=esend, dst_ref=yedge.at[d],
            send_sem=es_sem.at[d - 1], recv_sem=er_sem.at[d - 1],
            device_id={"member": partner(d)}, device_id_type=MESH,
        )

    others = range(peers - 1, 0, -1)
    edges = 2 * outn

    def gather_copy(m, part, d):
        return pltpu.make_async_remote_copy(
            src_ref=osend.at[m, :, parts[part]],
            dst_ref=ybuf.at[d, m, :, parts[part]],
            send_sem=as_sem.at[d - 1], recv_sem=ar_sem.at[d - 1],
            device_id={"member": partner(d)}, device_id_type=MESH,
        )

    def gather_whole(d):
        return pltpu.make_async_remote_copy(
            src_ref=osend, dst_ref=ybuf.at[d],
            send_sem=as_sem.at[d - 1], recv_sem=ar_sem.at[d - 1],
            device_id={"member": partner(d)}, device_id_type=MESH,
        )

    def project(m, part, values):
        for n, value in values:
            span = slice(n, n + chunk)
            value = dot(wo[...], value)
            outs[m, :, span] = value
            osend[m, :, span] = value.astype(BF16)
        for d in others:
            gather_copy(m, part, d).start()

    waiting = None
    for m in range(members):
        wide = widened(x, m, (-1, 0, 1))
        for part, range_of in enumerate(parts):
            values = []
            for n in range(range_of.start, range_of.stop, chunk):
                span = slice(n, n + chunk)
                total = convolve(wf, wide, span) + skip[m, :, span].astype(F32)
                put(m, span, total)
                pedge[m, :, span] = edge_rows(m, span)
                values.append((n, gelu_value(total).astype(BF16)))
            if waiting is not None:
                project(*waiting)
            waiting = (m, part, values)
    project(*waiting)

    halo_wait([(hs, hx, hs_sem, hx_sem)], "recv")
    halos = [stacked(hx[0, m], hx[1, m], (-1, 0, 1)) for m in range(members)]
    work = [(m, span) for m in range(members) for span in spans]
    totals, values = {}, {}
    for step in range(len(work) + 2):
        if step < len(work):
            m, span = work[step]
            totals[step] = pedge[m, :, span] + dot(wfh[...], halos[m][:, span])
        if 1 <= step <= len(work):
            m, span = work[step - 1]
            total = totals.pop(step - 1)
            put_edge_rows(m, span, total)
            values[step - 1] = gelu_value(total).astype(BF16)
        if step >= 2:
            m, span = work[step - 2]
            value = dot(woe[...], values.pop(step - 2))
            esend[m, :, span] = value.astype(BF16)
            oute[m * edges : (m + 1) * edges, span] = value
    for d in others:
        edge_copy(d).start()

    block = 8 * rows
    for m in range(members):
        for n in range(0, full, block):
            for span in spans:
                lines = slice(n, n + block)
                slope[m, lines, span] = gelu_slope(get(m, span, lines)).astype(BF16)
        extract_edges(m, slope[m], se)
    halo_start(se, hse, gs_sem, hg_sem)
    build_backward()
    build_edges(wbh, True)
    eye = (
        lax.broadcasted_iota(jnp.int32, (chans, chans), 0)
        == lax.broadcasted_iota(jnp.int32, (chans, chans), 1)
    ).astype(F32).astype(BF16)
    for k in range(outn):
        flat = jnp.broadcast_to(out_w[k : k + 1, :].astype(F32), (chunk, chans)).astype(BF16)
        wcol[k] = dot_nt(spread, flat).astype(BF16)
        wrow[k] = dot_nt(eye, flat[:lane])

    tgt.wait()
    total_members = peers * members
    for d in others:
        gather_whole(d).wait_recv()
    for part in range(2):
        for n in range(parts[part].start, parts[part].stop, chunk):
            span = slice(n, n + chunk)
            own = [outs[m, :, span] for m in range(members)]
            pairs = [smooth_slope(v - v) for v in own]
            for i in range(members):
                for j in range(i):
                    term = smooth_slope(own[i] - own[j])
                    pairs[i] = pairs[i] + term
                    pairs[j] = pairs[j] - term
            for d in range(1, peers):
                for j in range(members):
                    other = ybuf[d, j, :, span].astype(F32)
                    for i in range(members):
                        pairs[i] = pairs[i] + smooth_slope(own[i] - other)
            for i in range(members):
                grad = smooth_slope(own[i] - target[:, span]) - pairs[i] / (total_members - 1)
                for k in range(outn):
                    part_k = grad[k * rows : (k + 1) * rows]
                    gout[i, k, :, span] = part_k

    shape = (members * edges, edges)
    repeat = (
        split_index(shape, 0, edges)[1] == lax.broadcasted_iota(jnp.int32, shape, 1)
    ).astype(F32).astype(BF16)
    for m in range(members):
        for side in range(2):
            for k in range(outn):
                row = m * edges + side * outn + k
                from_row = k * rows + side * (rows - 1)
                tedge[row : row + 1, :] = target[from_row : from_row + 1, :]
    for d in others:
        edge_copy(d).wait_recv()
    for span in spans:
        own = oute[:, span]
        total = jnp.zeros(own.shape, F32)
        for j in range(members):
            other = jnp.concatenate([own[j * edges : (j + 1) * edges]] * members, axis=0)
            total = total + smooth_slope(own - other)
        for d in range(1, peers):
            for j in range(members):
                total = total + smooth_slope(own - dot(repeat, yedge[d, j, :, span]))
        grad = smooth_slope(own - tedge[:, span]) - total / (total_members - 1)
        grad = grad.astype(BF16).astype(F32)
        for i in range(members):
            for side in range(2):
                row = i * edges + side * outn
                gsend[side, i, :, span] = grad[row : row + outn]
                for k in range(outn):
                    line = side * (rows - 1)
                    gout[i, k, line : line + 1, span] = grad[row + k : row + k + 1]

    halo_start(gsend, hgo, cs_sem, cr_sem)
    def activate(m, span):
        score = [gout[m, k, :, span].astype(BF16) for k in range(outn)]
        for n in range(0, full, rows):
            lines = slice(n, n + rows)
            grad = wcol[0, lines, :] * score[0]
            for k in range(1, outn):
                grad = grad + wcol[k, lines, :] * score[k]
            act[m, lines, span] = grad * slope[m, lines, span]

    for m in range(members):
        for span in spans:
            activate(m, span)
        wide = widened(act, m, (1, 0, -1))
        for span in spans:
            put(m, span, convolve(wb, wide, span))
            pedge[m, :, span] = edge_rows(m, span)
    halo_wait([(hs, hx, hs_sem, hx_sem), (se, hse, gs_sem, hg_sem)], "send")
    for d in others:
        gather_whole(d).wait_send()
        edge_copy(d).wait_send()
    halo_wait([(se, hse, gs_sem, hg_sem), (gsend, hgo, cs_sem, cr_sem)], "recv")
    halos = []
    for m in range(members):
        both = []
        for half in range(2):
            tiles = []
            for c in range(0, cols, lane):
                span = slice(c, c + lane)
                grad = wrow[0] * hgo[half, m, 0:1, span]
                for k in range(1, outn):
                    grad = grad + wrow[k] * hgo[half, m, k : k + 1, span]
                tiles.append((grad * hse[half, m, :, span].astype(F32)).astype(BF16))
            both.append(jnp.concatenate(tiles, axis=1))
        halos.append(stacked(both[0], both[1], (1, 0, -1)))
    for step in range(len(work) + 1):
        if step < len(work):
            m, span = work[step]
            totals[step] = pedge[m, :, span] + dot(wbh[...], halos[m][:, span])
        if step >= 1:
            m, span = work[step - 1]
            put_edge_rows(m, span, totals.pop(step - 1))

    halo_wait([(gsend, hgo, cs_sem, cr_sem)], "send")


def finish(dims, pre, out_hbm, out, sem):
    members, cols, chunk = dims
    copies = []
    for m in range(members):
        for n in range(0, cols, chunk):
            span = slice(n, n + chunk)
            tiles = [pre[m, (n + k) // lane] for k in range(0, chunk, lane)]
            out[m, :, span] = jnp.concatenate(tiles, axis=1).astype(BF16)
            copy = pltpu.make_async_copy(
                out.at[m, :, span], out_hbm.at[m, :, span], sem.at[m, n // chunk]
            )
            copy.start()
            copies.append(copy)
    for copy in copies:
        copy.wait()


def local(features, skip, conv_weight, out_weight, target):
    members, chans, rows, cols = features.shape
    outn = out_weight.shape[0]
    peers = lax.axis_size("member")
    count = lax.axis_size("space")
    full = chans * rows
    chunk = min(cols, 256)
    dims = (members, chans, rows, cols, peers, count, outn, chunk)
    dma = pltpu.SemaphoreType.DMA
    anywhere = pl.BlockSpec(memory_space=pltpu.HBM)
    vmem = pl.BlockSpec(memory_space=pltpu.VMEM)
    held = pl.pallas_call(
        functools.partial(kernel, dims),
        out_shape=pltpu.VMEM((members, cols // lane, full, lane), F32),
        in_specs=[anywhere] * 5,
        out_specs=vmem,
        scratch_shapes=[
            pltpu.VMEM((members, full, cols), BF16),
            pltpu.VMEM((members, full, cols), BF16),
            pltpu.VMEM(conv_weight.shape, BF16),
            pltpu.VMEM(out_weight.shape, BF16),
            pltpu.VMEM((outn * rows, cols), F32),
            pltpu.VMEM((members, full, cols), BF16),
            pltpu.VMEM((members, full, cols), BF16),
            pltpu.VMEM((2, members, chans, cols), BF16),
            pltpu.VMEM((2, members, chans, cols), BF16),
            pltpu.VMEM((2, members, chans, cols), BF16),
            pltpu.VMEM((2, members, outn, cols), F32),
            pltpu.VMEM((members, outn * rows, cols), F32),
            pltpu.VMEM((members, outn * rows, cols), BF16),
            pltpu.VMEM((peers, members, outn * rows, cols), BF16),
            pltpu.VMEM((members, 2 * outn, cols), BF16),
            pltpu.VMEM((peers, members, 2 * outn, cols), BF16),
            pltpu.VMEM((members * 2 * outn, cols), F32),
            pltpu.VMEM((members * 2 * outn, cols), F32),
            pltpu.VMEM((members, 2 * chans, cols), F32),
            pltpu.VMEM((members, outn, rows, cols), F32),
            pltpu.VMEM((2, members, outn, cols), F32),
            pltpu.VMEM((2, members, chans, cols), BF16),
            pltpu.VMEM((full, 3 * full), BF16),
            pltpu.VMEM((2 * chans, 6 * chans), BF16),
            pltpu.VMEM((full, 3 * full), BF16),
            pltpu.VMEM((2 * chans, 6 * chans), BF16),
            pltpu.VMEM((3, full // lane, full, lane), F32),
            pltpu.VMEM((outn * rows, full), BF16),
            pltpu.VMEM((2 * outn, 2 * chans), BF16),
            pltpu.VMEM((outn, full, chunk), BF16),
            pltpu.VMEM((outn, chans, lane), F32),
            pltpu.VMEM((2 * chans, full), BF16),
            dma((members + 4,)),
            dma((2,)),
            dma((2,)),
            dma((2,)),
            dma((2,)),
            dma((peers - 1,)),
            dma((peers - 1,)),
            dma((peers - 1,)),
            dma((peers - 1,)),
            dma((2,)),
            dma((2,)),
        ],
        compiler_params=pltpu.CompilerParams(collective_id=0, has_side_effects=True, vmem_limit_bytes=58 * 2**20),
    )(
        features.reshape(members, full, cols),
        skip.reshape(members, full, cols),
        conv_weight,
        out_weight,
        target.reshape(outn * rows, cols),
    )
    result = pl.pallas_call(
        functools.partial(finish, (members, cols, chunk)),
        out_shape=jax.ShapeDtypeStruct((members, full, cols), BF16),
        in_specs=[vmem],
        out_specs=anywhere,
        scratch_shapes=[pltpu.VMEM((members, full, cols), BF16), dma((members, cols // chunk))],
        compiler_params=pltpu.CompilerParams(vmem_limit_bytes=16 * 2**20),
    )(held)
    return result.reshape(members, chans, rows, cols)


def solution(mesh):
    placed = (
        P("member", None, "space", None),
        P("member", None, "space", None),
        P(),
        P(),
        P(None, "space", None),
    )
    return jax.shard_map(
        local,
        mesh=mesh,
        in_specs=placed,
        out_specs=P("member", None, "space", None),
        check_vma=False,
    )
```
